256 devices in a mesh: ctx: 32 (over z, x), head: 4 (over y_hi, core), side: 2 (over y_lo).
Axes of the slice: x: 4, y: 4 (y_hi: 2, y_lo: 2; y = y_hi * 2 + y_lo), z: 8, core: 2. Of those that a mesh axis runs over, the one named last changes fastest.
Arguments:
- prefill_query: bfloat16 [8192, 64, 128], P('ctx', ('head', 'side')), may hold values from -6 to 6
- prefill_keys: bfloat16 [8192, 8, 128], P('ctx', ('head', 'side')), may hold values from -6 to 6
- prefill_values: bfloat16 [8192, 8, 128], P('ctx', ('head', 'side')), may hold values from -6 to 6
- token_pos: int32 [8192], P('ctx'), may hold values from 0 to 8191, as said below
- scale_exp: int32 [1024, 8, 2], P('ctx', ('head', 'side')), may hold values from -7 to -5
- page_owner: int32 [1024], P('ctx'), may hold values from 0 to 31, as said below
- draft_query: bfloat16 [256, 64, 128], P(None, ('head', 'side')), may hold values from -6 to 6
- draft_keys: bfloat16 [256, 8, 128], P('side', 'head'), may hold values from -6 to 6
- draft_values: bfloat16 [256, 8, 128], P('side', 'head'), may hold values from -6 to 6
- parents: int32 [256], replicated, may hold values from 0 to 254, as said below
Outputs:
- prefill_out: bfloat16 [8192, 64, 128], P('ctx', ('head', 'side'))
- cache_keys: bfloat16 [8192, 8, 128], P('ctx', ('head', 'side'))
- cache_values: bfloat16 [8192, 8, 128], P('ctx', ('head', 'side'))
- verify_out: bfloat16 [256, 64, 128], P('ctx', ('head', 'side'))
The draws below stay inside these ranges and needn't reach their ends.
Inputs may be any that keep to these rules, and one draw needn't show every extreme that they name: `token_pos`: a permutation of 0 to 8191; the rows of shard c of ctx hold the runs a and 2 * 32 - 1 - a of 128 consecutive positions, in order, with a different a for each shard. `page_owner`: the 1024 // 32 entries of one ctx shard are a permutation of 0 to 32 - 1. parents[0] = 0, and parents[r] < r for r >= 1.
All inputs are finite; a program needn't handle non-finite values.
Results may differ from the reference program's by a relative error of at most 0.0049.
Values may be sent and summed in bfloat16 or wider, within the bound.
No kernel may reach another device: no remote copies, remote signals or barrier semaphores. Data moves between devices by JAX's collectives and lax.ppermute only.
A program may use at most 64 MiB of HBM per device.

```python
import jax
import jax.numpy as jnp
import numpy as np
from jax import lax

HD = 128
QH = 64
KVH = 8
QG = 8
TOK_DEV = 256
TOKENS = 8192
PAGE = 8
PAGES = 1024
ROWS = 256
N_CTX = 32


def folded_positions(key):
    shard_count = TOKENS // TOK_DEV
    shard_order = jax.random.permutation(jax.random.fold_in(key, 7), shard_count)
    row_index = jnp.arange(TOKENS, dtype=jnp.int32)
    shard_of = row_index // TOK_DEV
    inside = row_index % TOK_DEV
    half_rows = TOK_DEV // 2
    first_piece = shard_order[shard_of]
    piece_index = jnp.where(inside < half_rows, first_piece, 2 * shard_count - 1 - first_piece)
    return (piece_index * half_rows + inside % half_rows).astype(jnp.int32)


def draw_token_pos(key, part):
    return folded_positions(key)


def draw_page_owner(key, part):
    shard_count = TOKENS // TOK_DEV
    shard_keys = jax.random.split(jax.random.fold_in(key, 5), shard_count)

    def one_shard(shard_key):
        return jax.random.permutation(shard_key, shard_count)
    return jax.vmap(one_shard)(shard_keys).reshape(-1).astype(jnp.int32)


def draw_parents(key, part):
    upper = jnp.maximum(jnp.arange(ROWS, dtype=jnp.int32), 1)
    return jax.random.randint(jax.random.fold_in(key, 3), (ROWS,), 0, upper).astype(jnp.int32)


def draw_prefill_query(key, part):
    shape = (TOKENS, QH, HD)
    field = jnp.clip(1.5 * jax.random.normal(key, shape, jnp.float32), -6.0, 6.0)
    return field.astype(jnp.bfloat16)


def draw_prefill_keys(key, part):
    shape = (TOKENS, KVH, HD)
    leading = draw_prefill_query(key, part).astype(jnp.float32)[:, ::QG]
    field = jax.random.normal(jax.random.fold_in(key, 29), shape, jnp.float32)
    field = jnp.clip(field + 0.6 * leading, -6.0, 6.0)
    return field.astype(jnp.bfloat16)


def draw_draft_query(key, part):
    shape = (ROWS, QH, HD)
    seeded = jax.random.fold_in(key, 37)
    field = jnp.clip(1.5 * jax.random.normal(seeded, shape, jnp.float32), -6.0, 6.0)
    return field.astype(jnp.bfloat16)


def draw_draft_keys(key, part):
    shape = (ROWS, KVH, HD)
    leading = draw_draft_query(key, part).astype(jnp.float32)[:, ::QG]
    field = jax.random.normal(jax.random.fold_in(key, 31), shape, jnp.float32)
    field = jnp.clip(field + 0.6 * leading, -6.0, 6.0)
    return field.astype(jnp.bfloat16)


def plant(values, own_key, low, largest):
    place = [jax.random.randint(jax.random.fold_in(own_key, axis), (), 0, length) for axis, length in enumerate(values.shape)]
    widest = values.shape.index(max(values.shape))
    beside = place[:widest] + [(place[widest] + 1) % values.shape[widest]] + place[widest + 1:]
    return values.at[tuple(place)].set(low).at[tuple(beside)].set(largest)


def shard_levels(stream_key, extent, pieces, smallest, top_value):
    factor_of, own = 1.0, jax.random.fold_in(stream_key, 6)
    for position, blocks in pieces:
        heights = jnp.exp(jax.random.uniform(jax.random.fold_in(own, position), (blocks,), jnp.float32, smallest / len(pieces), top_value / len(pieces)))
        factor_of = factor_of * jnp.repeat(heights, extent[position] // blocks).reshape([-1 if axis == position else 1 for axis in range(len(extent))])
    return factor_of


def noise(key, dims, spread, bound, pieces=(), kind=jnp.bfloat16):
    values = spread * jax.random.normal(key, dims, jnp.float32)
    if pieces:
        values = values * shard_levels(key, dims, pieces, -0.22, 0.18)
    return jnp.clip(values, -bound, bound).astype(kind)


def setup_inputs(seed: int = 0) -> dict:
    key_list = jax.random.split(jax.random.key(seed), 11)
    return {
        "prefill_query": draw_prefill_query(jax.random.fold_in(key_list[10], 71), 0),
        "prefill_keys": draw_prefill_keys(jax.random.fold_in(key_list[10], 71), 0),
        "prefill_values": noise(key_list[2], (TOKENS, KVH, HD), 1.0, 6.0, ((0, 32), (1, 8))),
        "token_pos": draw_token_pos(jax.random.fold_in(key_list[10], 71), 0),
        "scale_exp": plant(jax.random.randint(key_list[4], (PAGES, KVH, 2), -7, -4), jax.random.fold_in(key_list[4], 1), -7, (-4) - 1).astype(jnp.int32),
        "page_owner": draw_page_owner(jax.random.fold_in(key_list[10], 71), 0),
        "draft_query": draw_draft_query(jax.random.fold_in(key_list[10], 71), 0),
        "draft_keys": draw_draft_keys(jax.random.fold_in(key_list[10], 71), 0),
        "draft_values": noise(key_list[8], (ROWS, KVH, HD), 1.0, 6.0, ((0, 2), (1, 4))),
        "parents": draw_parents(jax.random.fold_in(key_list[10], 71), 0),
    }


NEG_FILL = -1.0e30
FP_LIMIT = 448.0
LOG_TWO_E = 1.4426950408889634


def power_two(exponent):
    levels = jnp.arange(-7, -4, dtype=jnp.int32)
    table = jnp.asarray(np.array([2.0 ** level for level in range(-7, -4)], np.float32))
    return jnp.sum(jnp.where(exponent[..., None] == levels, table, jnp.float32(0.0)), axis=-1)


def ancestors(parent_rows):
    row_total = parent_rows.shape[0]
    row_index = jnp.arange(row_total, dtype=jnp.int32)
    linked = ((parent_rows[:, None] == row_index[None, :]) | (row_index[:, None] == row_index[None, :])).astype(jnp.float32)
    for _ in range(row_total.bit_length()):
        linked = jnp.minimum(jnp.dot(linked, linked, precision=lax.Precision.HIGHEST), jnp.float32(1.0))
    return linked > 0.5


def reference(prefill_query, prefill_keys, prefill_values, token_pos, scale_exp, page_owner, draft_query, draft_keys, draft_values, parents):
    scale_factor = HD ** -0.5
    head_outputs = []
    for kv_head in range(KVH):
        head_keys = prefill_keys[:, kv_head]
        head_values = prefill_values[:, kv_head]
        query_blocks = prefill_query[:, kv_head * QG:(kv_head + 1) * QG].reshape(TOKENS // TOK_DEV, TOK_DEV * QG, HD)
        place_blocks = jnp.repeat(token_pos, QG).reshape(TOKENS // TOK_DEV, TOK_DEV * QG)

        def attend_block(item, head_keys=head_keys, head_values=head_values):
            query_rows, query_places = item
            scores = scale_factor * jnp.dot(query_rows, head_keys.T, preferred_element_type=jnp.float32)
            allowed = query_places[:, None] >= token_pos[None, :]
            row_top = jnp.ceil(LOG_TWO_E * jnp.max(jnp.where(allowed, scores, NEG_FILL), axis=1, keepdims=True))
            weights = jnp.where(allowed, jnp.exp2(LOG_TWO_E * scores - row_top), jnp.float32(0.0))
            numer = jnp.dot(weights.astype(jnp.bfloat16), head_values, preferred_element_type=jnp.float32)
            return (numer / jnp.sum(weights, axis=1, keepdims=True)).astype(jnp.bfloat16)

        head_outputs.append(lax.map(attend_block, (query_blocks, place_blocks)).reshape(TOKENS, QG, HD))
    prefill_out = jnp.concatenate(head_outputs, axis=1)

    limits = FP_LIMIT * power_two(scale_exp)
    row_limits = jnp.repeat(limits, PAGE, axis=0)
    deq_keys = jnp.clip(prefill_keys.astype(jnp.float32), -row_limits[..., 0:1], row_limits[..., 0:1]).astype(jnp.bfloat16)
    deq_values = jnp.clip(prefill_values.astype(jnp.float32), -row_limits[..., 1:2], row_limits[..., 1:2]).astype(jnp.bfloat16)
    shard_index = jnp.arange(N_CTX, dtype=jnp.int32)
    owners = page_owner.reshape(N_CTX, N_CTX)
    inverse = jnp.sum(jnp.where(owners[:, None, :] == shard_index[None, :, None], shard_index[None, None, :], 0), axis=2).astype(jnp.int32)

    def relayout(dequantized):
        paged = dequantized.reshape(N_CTX, N_CTX, PAGE, KVH, HD)
        picked = paged[shard_index[:, None], inverse]
        return jnp.transpose(picked, (1, 0, 2, 3, 4)).reshape(TOKENS, KVH, HD)

    cache_keys = relayout(deq_keys)
    cache_values = relayout(deq_values)

    tree_mask = jnp.repeat(ancestors(parents), QG, axis=0)
    verify_heads = []
    for kv_head in range(KVH):
        draft_rows = draft_query[:, kv_head * QG:(kv_head + 1) * QG].reshape(ROWS * QG, HD)
        cache_scores = scale_factor * jnp.dot(draft_rows, deq_keys[:, kv_head].T, preferred_element_type=jnp.float32)
        tree_scores = scale_factor * jnp.dot(draft_rows, draft_keys[:, kv_head].T, preferred_element_type=jnp.float32)
        row_max = jnp.maximum(jnp.max(cache_scores, axis=1, keepdims=True), jnp.max(jnp.where(tree_mask, tree_scores, NEG_FILL), axis=1, keepdims=True))
        row_top = jnp.ceil(LOG_TWO_E * row_max)
        cache_weights = jnp.exp2(LOG_TWO_E * cache_scores - row_top)
        tree_weights = jnp.where(tree_mask, jnp.exp2(LOG_TWO_E * tree_scores - row_top), jnp.float32(0.0))
        numer = jnp.dot(cache_weights.astype(jnp.bfloat16), deq_values[:, kv_head], preferred_element_type=jnp.float32)
        numer = numer + jnp.dot(tree_weights.astype(jnp.bfloat16), draft_values[:, kv_head], preferred_element_type=jnp.float32)
        total = jnp.sum(cache_weights, axis=1, keepdims=True) + jnp.sum(tree_weights, axis=1, keepdims=True)
        verify_heads.append((numer / total).astype(jnp.bfloat16).reshape(ROWS, QG, HD))
    verify_out = jnp.concatenate(verify_heads, axis=1)
    return (prefill_out, cache_keys, cache_values, verify_out)
```

```python
import functools

import jax
import jax.numpy as jnp
from jax import lax
from jax.experimental import pallas as pl
from jax.experimental.pallas import tpu as pltpu
from jax.sharding import Mesh
from jax.sharding import PartitionSpec as P

CTX = ("z", "x")
NEG = -1.0e30
LOG_TWO_E = 1.4426950408889634
TOK = 256
HALF = 128
GROUPS = 8
WIDTH = 128
PAGES = 32
META = 32
PAY = 2 * TOK + META
QH = HALF * GROUPS
SLOTS = 4
COEF = WIDTH**-0.5 * LOG_TWO_E
BF = jnp.bfloat16
F32 = jnp.float32


def iota(shape, dim):
    return lax.broadcasted_iota(jnp.int32, shape, dim)


def dot_t(a, b):
    return lax.dot_general(a, b, (((1,), (1,)), ((), ())), preferred_element_type=F32)


def dot(a, b):
    return jnp.dot(a, b, preferred_element_type=F32)


def held(x):
    return pltpu.with_memory_space_constraint(x, pltpu.VMEM)


def vmem(n):
    return [pl.BlockSpec(memory_space=pltpu.VMEM)] * n


def pack_kernel(pos_ref, scale_ref, owner_ref, k_ref, v_ref, out_ref):
    out_ref[0:TOK, :] = k_ref[...]
    out_ref[TOK : 2 * TOK, :] = v_ref[...]
    first = (pos_ref[0] // HALF).astype(F32)
    diag = iota((PAGES, PAGES), 0) == iota((PAGES, PAGES), 1)

    def column(row):
        return jnp.sum(jnp.where(diag, row, 0.0), axis=1, keepdims=True)

    scale = scale_ref[...]
    bound = jnp.where(scale == -7, 3.5, jnp.where(scale == -6, 7.0, 14.0)).astype(F32)
    lane = iota((META, WIDTH), 1)
    meta = jnp.where(
        lane < 32,
        column(bound[0:1, :]),
        jnp.where(
            lane < 64,
            column(bound[1:2, :]),
            jnp.where(lane < 96, column(owner_ref[...].astype(F32)), first),
        ),
    )
    out_ref[2 * TOK :, :] = meta.astype(BF)


def me_index():
    return lax.axis_index("z") * 4 + lax.axis_index("x")


def softmax_update(s, v, m_ref, acc_ref, rows):
    keys = s.shape[1]
    top = jnp.broadcast_to(jnp.max(s, axis=1, keepdims=True), (s.shape[0], WIDTH))
    old = m_ref[rows, :]
    new = jnp.maximum(old, jnp.ceil(top))
    factor = jnp.exp2(old - new)
    p = jnp.exp2(s - jnp.tile(new, (1, keys // WIDTH))).astype(BF)
    acc_ref[rows, :] = acc_ref[rows, :] * jnp.tile(factor, (1, 2)) + dot(p, v)
    m_ref[rows, :] = new


def softmax_start(s, v, m_ref, acc_ref, rows):
    keys = s.shape[1]
    top = jnp.broadcast_to(jnp.max(s, axis=1, keepdims=True), (s.shape[0], WIDTH))
    new = jnp.ceil(top)
    p = jnp.exp2(s - jnp.tile(new, (1, keys // WIDTH))).astype(BF)
    acc_ref[rows, :] = dot(p, v)
    m_ref[rows, :] = new


def with_ones(v):
    return jnp.concatenate([v, jnp.ones(v.shape, BF)], axis=1)


def clipped_source(src_ref, base, col, mine, kc_ref, vc_ref, slot, ck_ref, cv_ref):
    meta = src_ref[base + 2 * TOK : base + PAY, :]
    pick = iota((WIDTH, 3 * WIDTH), 0) == (iota((WIDTH, 3 * WIDTH), 1) // WIDTH) * 32
    spread = dot(meta, pick.astype(BF)).astype(BF)
    grow = (iota((TOK, META), 0) // 8 == iota((TOK, META), 1)).astype(BF)
    rows = dot(grow, spread)
    k = src_ref[base : base + TOK, :].astype(F32)
    v = src_ref[base + TOK : base + 2 * TOK, :].astype(F32)
    kb, vb, own = rows[:, :WIDTH], rows[:, WIDTH : 2 * WIDTH], rows[:, 2 * WIDTH :]
    k = jnp.maximum(jnp.minimum(k, kb), -kb)
    v = jnp.maximum(jnp.minimum(v, vb), -vb)
    kc_ref[slot * TOK : (slot + 1) * TOK, :] = k.astype(BF)
    vc_ref[slot * TOK : (slot + 1) * TOK, :] = with_ones(v.astype(BF))
    hit = own == mine.astype(F32)
    at = pl.ds(pl.multiple_of(col * 8, 8), 8)
    ck_ref[at, :] = jnp.sum(jnp.where(hit, k, 0.0).reshape(PAGES, 8, WIDTH), axis=0)
    cv_ref[at, :] = jnp.sum(jnp.where(hit, v, 0.0).reshape(PAGES, 8, WIDTH), axis=0)


def first_of(src_ref, base):
    meta = src_ref[base + 2 * TOK : base + PAY, :].astype(F32)
    return jnp.max(meta[:, 96:]).astype(jnp.int32)


def own_kernel(
    q_ref, own_ref, dq_ref, tree_ref, far_ref, par_ref,
    mh_ref, ah_ref, ml_ref, al_ref, mv_ref, av_ref, ck_ref, cv_ref,
    kc_ref, vc_ref,
):
    me = me_index()
    side = lax.axis_index("side")
    first = first_of(own_ref, 0)
    swap = (first >= PAGES).astype(jnp.int32)
    lo = pl.multiple_of(swap * HALF, HALF)
    hi = pl.multiple_of(HALF - swap * HALF, HALF)
    k_lo, k_hi = own_ref[pl.ds(lo, HALF), :], own_ref[pl.ds(hi, HALF), :]
    v_lo = with_ones(own_ref[pl.ds(pl.multiple_of(TOK + lo, HALF), HALF), :])
    v_hi = with_ones(own_ref[pl.ds(pl.multiple_of(TOK + hi, HALF), HALF), :])
    k_both = jnp.concatenate([k_lo, k_hi], axis=0)
    v_both = jnp.concatenate([v_lo, v_hi], axis=0)
    part = 256
    for t in range(QH // part):
        rows = pl.ds(t * part, part)
        token = iota((part, HALF), 0) // GROUPS + t * part // GROUPS
        open_ = iota((part, HALF), 1) <= token
        q = q_ref[pl.ds(pl.multiple_of(hi * GROUPS + t * part, part), part), :]
        s = dot_t(q, k_both) * COEF
        s = jnp.concatenate([s[:, :HALF], jnp.where(open_, s[:, HALF:], NEG)], axis=1)
        softmax_start(s, v_both, mh_ref, ah_ref, rows)
        q = q_ref[pl.ds(pl.multiple_of(lo * GROUPS + t * part, part), part), :]
        s = jnp.where(open_, dot_t(q, k_lo) * COEF, NEG)
        softmax_start(s, v_lo, ml_ref, al_ref, rows)

    link = (par_ref[...] == iota((TOK, TOK), 0)) | (iota((TOK, TOK), 0) == iota((TOK, TOK), 1))
    link = link.astype(F32).astype(BF)
    for _ in range(8):
        link = jnp.minimum(dot(link, link), 1.0).astype(BF)
    rows64 = GROUPS * 8
    take = (iota((rows64, TOK), 1) == me * 8 + iota((rows64, TOK), 0) // GROUPS).astype(F32).astype(BF)
    allowed = dot_t(take, link) > 0.5

    def head(ref, at):
        zero, one = ref[:, at : at + WIDTH], ref[:, at + WIDTH : at + 2 * WIDTH]
        return jnp.where(side == 0, zero, one)

    def rows_of(at):
        near, far = head(tree_ref, at), head(far_ref, at)
        return jnp.concatenate(
            [jnp.where(side == 0, near, far), jnp.where(side == 0, far, near)], axis=0
        )

    dq = dq_ref[pl.ds(pl.multiple_of(me * rows64, rows64), rows64), :]
    s = jnp.where(allowed, dot_t(dq, rows_of(0)) * COEF, NEG)
    softmax_start(s, with_ones(rows_of(2 * WIDTH)), mv_ref, av_ref, pl.ds(0, rows64))
    clipped_source(own_ref, 0, me, me, kc_ref, vc_ref, 0, ck_ref, cv_ref)
    s = dot_t(dq, kc_ref[...]) * COEF
    softmax_update(s, vc_ref[...], mv_ref, av_ref, pl.ds(0, rows64))


def flash_chunks(q_ref, q_at, k_ref, v_ref, base, chunks, m_ref, acc_ref):
    part = 256
    span = SLOTS * HALF

    def chunk(i, _):
        at = pl.multiple_of(base * HALF + i * span, HALF)
        k = k_ref[pl.ds(at, span), :]
        v = v_ref[pl.ds(at, span), :]
        for t in range(QH // part):
            q = q_ref[pl.ds(pl.multiple_of(q_at + t * part, part), part), :]
            softmax_update(dot_t(q, k) * COEF, v, m_ref, acc_ref, pl.ds(t * part, part))
        return 0

    lax.fori_loop(0, chunks, chunk, 0)


def step_kernel(layout, last, *refs):
    n_in = len(layout)
    q_ref, own_ref, dq_ref = refs[:3]
    srcs = refs[3 : 3 + n_in]
    state = refs[11 + n_in : 19 + n_in]
    if last:
        out_ref, ver_ref, ok_ref, ov_ref = refs[19 + n_in : 23 + n_in]
    kk_ref, vv_ref, kc_ref, vc_ref = refs[-4:]
    mh_ref, ah_ref, ml_ref, al_ref, mv_ref, av_ref, ck_ref, cv_ref = state
    me, z, x = me_index(), lax.axis_index("z"), lax.axis_index("x")
    first = first_of(own_ref, 0)
    swap = (first >= PAGES).astype(jnp.int32)
    mine = jnp.minimum(first, 2 * PAGES - 1 - first)
    blocks = [(r, i * PAY, d) for r, ds in zip(srcs, layout) for i, d in enumerate(ds)]
    n = len(blocks)
    lo_base = 2 * n + SLOTS
    n_hi, n_lo = jnp.int32(0), jnp.int32(0)
    for i, (ref, base, _) in enumerate(blocks):
        f = first_of(ref, base)
        other = (f >= PAGES).astype(jnp.int32)
        later = (jnp.minimum(f, 2 * PAGES - 1 - f) > mine).astype(jnp.int32)
        lo = base + other * HALF
        hi = base + HALF - other * HALF
        sel = jnp.where(later == 1, hi, lo)
        to = jnp.where(later == 1, n + n_hi, lo_base + n_lo)
        kk_ref[i * HALF : (i + 1) * HALF, :] = ref[pl.ds(pl.multiple_of(lo, 32), HALF), :]
        vv_ref[i * HALF : (i + 1) * HALF, :] = with_ones(
            ref[pl.ds(pl.multiple_of(lo + TOK, 32), HALF), :]
        )
        at = pl.ds(pl.multiple_of(to * HALF, HALF), HALF)
        kk_ref[at, :] = ref[pl.ds(pl.multiple_of(sel, 32), HALF), :]
        vv_ref[at, :] = with_ones(ref[pl.ds(pl.multiple_of(sel + TOK, 32), HALF), :])
        n_hi, n_lo = n_hi + later, n_lo + 1 - later
    for start, count in ((0, n + n_hi), (lo_base, n_lo)):
        for j in range(SLOTS - 1):
            at = pl.ds(pl.multiple_of((start + count + j) * HALF, HALF), HALF)
            kk_ref[at, :] = kk_ref[start * HALF : (start + 1) * HALF, :]
            vv_ref[at, :] = jnp.zeros((HALF, 2 * WIDTH), BF)
    q_lo = swap * QH
    q_hi = QH - swap * QH
    flash_chunks(q_ref, q_hi, kk_ref, vv_ref, 0, (n + n_hi + SLOTS - 1) // SLOTS, mh_ref, ah_ref)
    flash_chunks(q_ref, q_lo, kk_ref, vv_ref, lo_base, (n_lo + SLOTS - 1) // SLOTS, ml_ref, al_ref)

    for i, (ref, base, (dz, dx)) in enumerate(blocks):
        col = ((z + dz + 8) % 8) * 4 + (x + dx + 4) % 4
        clipped_source(ref, base, col, me, kc_ref, vc_ref, i, ck_ref, cv_ref)
    rows64 = GROUPS * 8
    dq = dq_ref[pl.ds(pl.multiple_of(me * rows64, rows64), rows64), :]
    softmax_update(dot_t(dq, kc_ref[...]) * COEF, vc_ref[...], mv_ref, av_ref, pl.ds(0, rows64))
    if last:
        part = 256
        for t in range(QH // part):
            rows = pl.ds(t * part, part)
            for at, acc in ((q_hi, ah_ref), (q_lo, al_ref)):
                a = acc[rows, :]
                out_ref[pl.ds(pl.multiple_of(at + t * part, part), part), :] = (
                    a[:, :WIDTH] / a[:, WIDTH:]
                ).astype(BF)
        a = av_ref[...]
        ver_ref[...] = (a[:, :WIDTH] / a[:, WIDTH:]).astype(BF)
        ok_ref[...] = ck_ref[...].astype(BF)
        ov_ref[...] = cv_ref[...].astype(BF)


STATE = [
    pltpu.VMEM((QH, WIDTH), F32),
    pltpu.VMEM((QH, 2 * WIDTH), F32),
    pltpu.VMEM((QH, WIDTH), F32),
    pltpu.VMEM((QH, 2 * WIDTH), F32),
    pltpu.VMEM((64, WIDTH), F32),
    pltpu.VMEM((64, 2 * WIDTH), F32),
    pltpu.VMEM((TOK, WIDTH), F32),
    pltpu.VMEM((TOK, WIDTH), F32),
]
GRANT = pltpu.CompilerParams(vmem_limit_bytes=40 * 1024 * 1024)


def cost(n):
    return pl.CostEstimate(
        flops=n * 4 * TOK * QH * WIDTH, bytes_accessed=n * PAY * WIDTH * 2, transcendentals=0
    )


def step(q, own, dq, sources, layout, state, last=False):
    n = sum(len(d) for d in layout)
    outs = STATE
    alias = {3 + len(layout) + i: i for i in range(8)}
    if last:
        outs = STATE + [
            jax.ShapeDtypeStruct((2 * QH, WIDTH), BF),
            jax.ShapeDtypeStruct((64, WIDTH), BF),
            jax.ShapeDtypeStruct((TOK, WIDTH), BF),
            jax.ShapeDtypeStruct((TOK, WIDTH), BF),
        ]
    slots = 3 * n + 2 * SLOTS
    return pl.pallas_call(
        functools.partial(step_kernel, layout, last),
        out_shape=outs,
        in_specs=vmem(11 + len(layout)),
        out_specs=vmem(len(outs)),
        scratch_shapes=[
            pltpu.VMEM((slots * HALF, WIDTH), BF),
            pltpu.VMEM((slots * HALF, 2 * WIDTH), BF),
            pltpu.VMEM((n * TOK, WIDTH), BF),
            pltpu.VMEM((n * TOK, 2 * WIDTH), BF),
        ],
        input_output_aliases=alias,
        cost_estimate=cost(n),
        compiler_params=GRANT,
        name=f"step{n}",
    )(*(held(a) for a in (q, own, dq, *sources, *state)))


def shift(b, axis, d):
    n = lax.axis_size(axis)
    return lax.ppermute(b, axis, [(i, (i + d) % n) for i in range(n)])


def body(
    prefill_query, prefill_keys, prefill_values, token_pos, scale_exp, page_owner,
    draft_query, draft_keys, draft_values, parents,
):
    q = prefill_query.reshape(2 * QH, WIDTH)
    dq = draft_query.reshape(2 * QH, WIDTH)
    own = pl.pallas_call(
        pack_kernel,
        out_shape=pltpu.VMEM((PAY, WIDTH), BF),
        compiler_params=pltpu.CompilerParams(vmem_limit_bytes=4 * 1024 * 1024),
        in_specs=[pl.BlockSpec(memory_space=pltpu.SMEM)] + vmem(4),
        out_specs=vmem(1)[0],
        name="pack",
    )(
        token_pos,
        jnp.transpose(scale_exp, (1, 2, 0)).reshape(2, PAGES),
        page_owner.reshape(1, PAGES),
        prefill_keys.reshape(TOK, WIDTH),
        prefill_values.reshape(TOK, WIDTH),
    )
    tree = jnp.concatenate(
        [draft_keys.reshape(HALF, 2 * WIDTH), draft_values.reshape(HALF, 2 * WIDTH)], axis=1
    )
    xs = [shift(own, "x", 1), shift(own, "x", -1), shift(own, "x", 2)]
    far = shift(tree, "side", 1)
    near_x = jnp.concatenate(xs, axis=0)
    state = pl.pallas_call(
        own_kernel,
        out_shape=STATE,
        in_specs=vmem(6),
        out_specs=vmem(8),
        scratch_shapes=[pltpu.VMEM((TOK, WIDTH), BF), pltpu.VMEM((TOK, 2 * WIDTH), BF)],
        cost_estimate=cost(2),
        compiler_params=GRANT,
        name="own",
    )(*(held(a) for a in (q, own, dq, tree, far)), parents.reshape(1, TOK))
    dxs = (-1, 1, 2)
    state = step(q, own, dq, [near_x], [[(0, d) for d in dxs]], state)
    ra = la = own
    rb = lb = near_x
    for s in range(1, 4):
        ra, la = shift(ra, "z", 1), shift(la, "z", -1)
        rb, lb = shift(rb, "z", 1), shift(lb, "z", -1)
        state = step(
            q, own, dq, [ra, la, rb, lb],
            [[(-s, 0)], [(s, 0)], [(-s, d) for d in dxs], [(s, d) for d in dxs]],
            state,
        )
    oa = shift(la, "z", -1)
    ob = shift(rb[: 2 * PAY], "z", 1)
    oc = shift(lb[2 * PAY :], "z", -1)
    out, ver, ck, cv = step(
        q, own, dq, [oa, ob, oc],
        [[(4, 0)], [(4, d) for d in dxs[:2]], [(4, dxs[2])]],
        state, last=True,
    )[8:]
    return (
        out.reshape(TOK, GROUPS, WIDTH),
        ck.reshape(TOK, 1, WIDTH),
        cv.reshape(TOK, 1, WIDTH),
        ver.reshape(8, GROUPS, WIDTH),
    )


def solution(mesh):
    finer = Mesh(
        mesh.devices.reshape(8, 4, mesh.shape["head"], mesh.shape["side"]),
        ("z", "x", "head", "side"),
    )
    full = P(CTX, ("head", "side"), None)
    in_specs = (
        full, full, full, P(CTX), full, P(CTX),
        P(None, ("head", "side"), None),
        P("side", "head", None), P("side", "head", None), P(),
    )
    return jax.shard_map(
        body, mesh=finer, in_specs=in_specs, out_specs=(full, full, full, full), check_vma=False
    )
```

```python
import functools

import jax
import jax.numpy as jnp
from jax import lax
from jax.experimental import pallas as pl
from jax.experimental.pallas import tpu as pltpu
from jax.sharding import Mesh
from jax.sharding import PartitionSpec as P


CTX = ("z", "x")
NEG = -1.0e30
LOG_TWO_E = 1.4426950408889634
TOK = 256
HALF = 128
GROUPS = 8
WIDTH = 128
PAGES = 32
META = 32
PAY = 2 * TOK + META
QH = HALF * GROUPS
SLOTS = 4
COEF = WIDTH**-0.5 * LOG_TWO_E
BF = jnp.bfloat16
F32 = jnp.float32


def iota(shape, dim):
    return lax.broadcasted_iota(jnp.int32, shape, dim)


def dot_t(a, b):
    return lax.dot_general(a, b, (((1,), (1,)), ((), ())), preferred_element_type=F32)


def dot(a, b):
    return jnp.dot(a, b, preferred_element_type=F32)


def held(x):
    return pltpu.with_memory_space_constraint(x, pltpu.VMEM)


def vmem(n):
    return [pl.BlockSpec(memory_space=pltpu.VMEM)] * n


def pack_kernel(pos_ref, scale_ref, owner_ref, k_ref, v_ref, out_ref):
    out_ref[0:TOK, :] = k_ref[...]
    out_ref[TOK : 2 * TOK, :] = v_ref[...]
    first = (pos_ref[0] // HALF).astype(F32)
    diag = iota((PAGES, PAGES), 0) == iota((PAGES, PAGES), 1)

    def column(row):
        return jnp.sum(jnp.where(diag, row, 0.0), axis=1, keepdims=True)

    scale = scale_ref[...]
    bound = jnp.where(scale == -7, 3.5, jnp.where(scale == -6, 7.0, 14.0)).astype(F32)
    lane = iota((META, WIDTH), 1)
    meta = jnp.where(
        lane < 32,
        column(bound[0:1, :]),
        jnp.where(
            lane < 64,
            column(bound[1:2, :]),
            jnp.where(lane < 96, column(owner_ref[...].astype(F32)), first),
        ),
    )
    out_ref[2 * TOK :, :] = meta.astype(BF)


def me_index():
    return lax.axis_index("z") * 4 + lax.axis_index("x")


def softmax_update(s, v, m_ref, acc_ref, rows):
    keys = s.shape[1]
    top = jnp.broadcast_to(jnp.max(s, axis=1, keepdims=True), (s.shape[0], WIDTH))
    old = m_ref[rows, :]
    new = jnp.maximum(old, jnp.ceil(top))
    factor = jnp.exp2(old - new)
    p = jnp.exp2(s - jnp.tile(new, (1, keys // WIDTH))).astype(BF)
    acc_ref[rows, :] = acc_ref[rows, :] * jnp.tile(factor, (1, 2)) + dot(p, v)
    m_ref[rows, :] = new


def softmax_start(s, v, m_ref, acc_ref, rows):
    keys = s.shape[1]
    top = jnp.broadcast_to(jnp.max(s, axis=1, keepdims=True), (s.shape[0], WIDTH))
    new = jnp.ceil(top)
    p = jnp.exp2(s - jnp.tile(new, (1, keys // WIDTH))).astype(BF)
    acc_ref[rows, :] = dot(p, v)
    m_ref[rows, :] = new


def with_ones(v):
    return jnp.concatenate([v, jnp.ones(v.shape, BF)], axis=1)


def clipped_source(src_ref, base, col, mine, kc_ref, vc_ref, slot, ck_ref, cv_ref):
    meta = src_ref[base + 2 * TOK : base + PAY, :]
    pick = iota((WIDTH, 3 * WIDTH), 0) == (iota((WIDTH, 3 * WIDTH), 1) // WIDTH) * 32
    spread = dot(meta, pick.astype(BF)).astype(BF)
    grow = (iota((TOK, META), 0) // 8 == iota((TOK, META), 1)).astype(BF)
    rows = dot(grow, spread)
    k = src_ref[base : base + TOK, :].astype(F32)
    v = src_ref[base + TOK : base + 2 * TOK, :].astype(F32)
    kb, vb, own = rows[:, :WIDTH], rows[:, WIDTH : 2 * WIDTH], rows[:, 2 * WIDTH :]
    k = jnp.maximum(jnp.minimum(k, kb), -kb)
    v = jnp.maximum(jnp.minimum(v, vb), -vb)
    kc_ref[slot * TOK : (slot + 1) * TOK, :] = k.astype(BF)
    vc_ref[slot * TOK : (slot + 1) * TOK, :] = with_ones(v.astype(BF))
    hit = own == mine.astype(F32)
    at = pl.ds(pl.multiple_of(col * 8, 8), 8)
    ck_ref[at, :] = jnp.sum(jnp.where(hit, k, 0.0).reshape(PAGES, 8, WIDTH), axis=0)
    cv_ref[at, :] = jnp.sum(jnp.where(hit, v, 0.0).reshape(PAGES, 8, WIDTH), axis=0)


def first_of(src_ref, base):
    meta = src_ref[base + 2 * TOK : base + PAY, :].astype(F32)
    return jnp.max(meta[:, 96:]).astype(jnp.int32)


def own_kernel(
    q_ref, own_ref, dq_ref, tree_ref, far_ref, par_ref,
    mh_ref, ah_ref, ml_ref, al_ref, mv_ref, av_ref, ck_ref, cv_ref,
    kc_ref, vc_ref,
):
    me = me_index()
    side = lax.axis_index("side")
    first = first_of(own_ref, 0)
    swap = (first >= PAGES).astype(jnp.int32)
    lo = pl.multiple_of(swap * HALF, HALF)
    hi = pl.multiple_of(HALF - swap * HALF, HALF)
    k_lo, k_hi = own_ref[pl.ds(lo, HALF), :], own_ref[pl.ds(hi, HALF), :]
    v_lo = with_ones(own_ref[pl.ds(pl.multiple_of(TOK + lo, HALF), HALF), :])
    v_hi = with_ones(own_ref[pl.ds(pl.multiple_of(TOK + hi, HALF), HALF), :])
    k_both = jnp.concatenate([k_lo, k_hi], axis=0)
    v_both = jnp.concatenate([v_lo, v_hi], axis=0)
    part = 256
    for t in range(QH // part):
        rows = pl.ds(t * part, part)
        token = iota((part, HALF), 0) // GROUPS + t * part // GROUPS
        open_ = iota((part, HALF), 1) <= token
        q = q_ref[pl.ds(pl.multiple_of(hi * GROUPS + t * part, part), part), :]
        s = dot_t(q, k_both) * COEF
        s = jnp.concatenate([s[:, :HALF], jnp.where(open_, s[:, HALF:], NEG)], axis=1)
        softmax_start(s, v_both, mh_ref, ah_ref, rows)
        q = q_ref[pl.ds(pl.multiple_of(lo * GROUPS + t * part, part), part), :]
        s = jnp.where(open_, dot_t(q, k_lo) * COEF, NEG)
        softmax_start(s, v_lo, ml_ref, al_ref, rows)

    link = (par_ref[...] == iota((TOK, TOK), 0)) | (iota((TOK, TOK), 0) == iota((TOK, TOK), 1))
    link = link.astype(F32).astype(BF)
    for _ in range(8):
        link = jnp.minimum(dot(link, link), 1.0).astype(BF)
    rows64 = GROUPS * 8
    take = (iota((rows64, TOK), 1) == me * 8 + iota((rows64, TOK), 0) // GROUPS).astype(F32).astype(BF)
    allowed = dot_t(take, link) > 0.5

    def head(ref, at):
        zero, one = ref[:, at : at + WIDTH], ref[:, at + WIDTH : at + 2 * WIDTH]
        return jnp.where(side == 0, zero, one)

    def rows_of(at):
        near, far = head(tree_ref, at), head(far_ref, at)
        return jnp.concatenate(
            [jnp.where(side == 0, near, far), jnp.where(side == 0, far, near)], axis=0
        )

    dq = dq_ref[pl.ds(pl.multiple_of(me * rows64, rows64), rows64), :]
    s = jnp.where(allowed, dot_t(dq, rows_of(0)) * COEF, NEG)
    softmax_start(s, with_ones(rows_of(2 * WIDTH)), mv_ref, av_ref, pl.ds(0, rows64))
    clipped_source(own_ref, 0, me, me, kc_ref, vc_ref, 0, ck_ref, cv_ref)
    s = dot_t(dq, kc_ref[...]) * COEF
    softmax_update(s, vc_ref[...], mv_ref, av_ref, pl.ds(0, rows64))


def flash_chunks(q_ref, q_at, k_ref, v_ref, base, chunks, m_ref, acc_ref):
    part = 256
    span = SLOTS * HALF

    def chunk(i, _):
        at = pl.multiple_of(base * HALF + i * span, HALF)
        k = k_ref[pl.ds(at, span), :]
        v = v_ref[pl.ds(at, span), :]
        for t in range(QH // part):
            q = q_ref[pl.ds(pl.multiple_of(q_at + t * part, part), part), :]
            softmax_update(dot_t(q, k) * COEF, v, m_ref, acc_ref, pl.ds(t * part, part))
        return 0

    lax.fori_loop(0, chunks, chunk, 0)


def step_kernel(layout, last, *refs):
    n_in = len(layout)
    q_ref, own_ref, dq_ref = refs[:3]
    srcs = refs[3 : 3 + n_in]
    state = refs[11 + n_in : 19 + n_in]
    if last:
        out_ref, ver_ref, ok_ref, ov_ref = refs[19 + n_in : 23 + n_in]
    kk_ref, vv_ref, kc_ref, vc_ref = refs[-4:]
    mh_ref, ah_ref, ml_ref, al_ref, mv_ref, av_ref, ck_ref, cv_ref = state
    me, z, x = me_index(), lax.axis_index("z"), lax.axis_index("x")
    first = first_of(own_ref, 0)
    swap = (first >= PAGES).astype(jnp.int32)
    mine = jnp.minimum(first, 2 * PAGES - 1 - first)
    blocks = [(r, i * PAY, d) for r, ds in zip(srcs, layout) for i, d in enumerate(ds)]
    n = len(blocks)
    lo_base = 2 * n + SLOTS
    n_hi, n_lo = jnp.int32(0), jnp.int32(0)
    for i, (ref, base, _) in enumerate(blocks):
        f = first_of(ref, base)
        other = (f >= PAGES).astype(jnp.int32)
        later = (jnp.minimum(f, 2 * PAGES - 1 - f) > mine).astype(jnp.int32)
        lo = base + other * HALF
        hi = base + HALF - other * HALF
        sel = jnp.where(later == 1, hi, lo)
        to = jnp.where(later == 1, n + n_hi, lo_base + n_lo)
        kk_ref[i * HALF : (i + 1) * HALF, :] = ref[pl.ds(pl.multiple_of(lo, 32), HALF), :]
        vv_ref[i * HALF : (i + 1) * HALF, :] = with_ones(
            ref[pl.ds(pl.multiple_of(lo + TOK, 32), HALF), :]
        )
        at = pl.ds(pl.multiple_of(to * HALF, HALF), HALF)
        kk_ref[at, :] = ref[pl.ds(pl.multiple_of(sel, 32), HALF), :]
        vv_ref[at, :] = with_ones(ref[pl.ds(pl.multiple_of(sel + TOK, 32), HALF), :])
        n_hi, n_lo = n_hi + later, n_lo + 1 - later
    for start, count in ((0, n + n_hi), (lo_base, n_lo)):
        for j in range(SLOTS - 1):
            at = pl.ds(pl.multiple_of((start + count + j) * HALF, HALF), HALF)
            kk_ref[at, :] = kk_ref[start * HALF : (start + 1) * HALF, :]
            vv_ref[at, :] = jnp.zeros((HALF, 2 * WIDTH), BF)
    q_lo = swap * QH
    q_hi = QH - swap * QH
    flash_chunks(q_ref, q_hi, kk_ref, vv_ref, 0, (n + n_hi + SLOTS - 1) // SLOTS, mh_ref, ah_ref)
    flash_chunks(q_ref, q_lo, kk_ref, vv_ref, lo_base, (n_lo + SLOTS - 1) // SLOTS, ml_ref, al_ref)

    for i, (ref, base, (dz, dx)) in enumerate(blocks):
        col = ((z + dz + 8) % 8) * 4 + (x + dx + 4) % 4
        clipped_source(ref, base, col, me, kc_ref, vc_ref, i, ck_ref, cv_ref)
    rows64 = GROUPS * 8
    dq = dq_ref[pl.ds(pl.multiple_of(me * rows64, rows64), rows64), :]
    softmax_update(dot_t(dq, kc_ref[...]) * COEF, vc_ref[...], mv_ref, av_ref, pl.ds(0, rows64))
    if last:
        part = 256
        for t in range(QH // part):
            rows = pl.ds(t * part, part)
            for at, acc in ((q_hi, ah_ref), (q_lo, al_ref)):
                a = acc[rows, :]
                out_ref[pl.ds(pl.multiple_of(at + t * part, part), part), :] = (
                    a[:, :WIDTH] / a[:, WIDTH:]
                ).astype(BF)
        a = av_ref[...]
        ver_ref[...] = (a[:, :WIDTH] / a[:, WIDTH:]).astype(BF)
        ok_ref[...] = ck_ref[...].astype(BF)
        ov_ref[...] = cv_ref[...].astype(BF)


STATE = [
    pltpu.VMEM((QH, WIDTH), F32),
    pltpu.VMEM((QH, 2 * WIDTH), F32),
    pltpu.VMEM((QH, WIDTH), F32),
    pltpu.VMEM((QH, 2 * WIDTH), F32),
    pltpu.VMEM((64, WIDTH), F32),
    pltpu.VMEM((64, 2 * WIDTH), F32),
    pltpu.VMEM((TOK, WIDTH), F32),
    pltpu.VMEM((TOK, WIDTH), F32),
]
GRANT = pltpu.CompilerParams(vmem_limit_bytes=40 * 1024 * 1024)


def cost(n):
    return pl.CostEstimate(
        flops=n * 4 * TOK * QH * WIDTH, bytes_accessed=n * PAY * WIDTH * 2, transcendentals=0
    )


def step(q, own, dq, sources, layout, state, last=False):
    n = sum(len(d) for d in layout)
    outs = STATE
    alias = {3 + len(layout) + i: i for i in range(8)}
    if last:
        outs = STATE + [
            jax.ShapeDtypeStruct((2 * QH, WIDTH), BF),
            jax.ShapeDtypeStruct((64, WIDTH), BF),
            jax.ShapeDtypeStruct((TOK, WIDTH), BF),
            jax.ShapeDtypeStruct((TOK, WIDTH), BF),
        ]
    slots = 3 * n + 2 * SLOTS
    return pl.pallas_call(
        functools.partial(step_kernel, layout, last),
        out_shape=outs,
        in_specs=vmem(11 + len(layout)),
        out_specs=vmem(len(outs)),
        scratch_shapes=[
            pltpu.VMEM((slots * HALF, WIDTH), BF),
            pltpu.VMEM((slots * HALF, 2 * WIDTH), BF),
            pltpu.VMEM((n * TOK, WIDTH), BF),
            pltpu.VMEM((n * TOK, 2 * WIDTH), BF),
        ],
        input_output_aliases=alias,
        cost_estimate=cost(n),
        compiler_params=GRANT,
    )(*(held(a) for a in (q, own, dq, *sources, *state)))


def shift(b, axis, d):
    n = lax.axis_size(axis)
    return lax.ppermute(b, axis, [(i, (i + d) % n) for i in range(n)])


def work(
    prefill_query, prefill_keys, prefill_values, token_pos, scale_exp, page_owner,
    draft_query, draft_keys, draft_values, parents,
):
    q = prefill_query.reshape(2 * QH, WIDTH)
    dq = draft_query.reshape(2 * QH, WIDTH)
    own = pl.pallas_call(
        pack_kernel,
        out_shape=pltpu.VMEM((PAY, WIDTH), BF),
        compiler_params=pltpu.CompilerParams(vmem_limit_bytes=4 * 1024 * 1024),
        in_specs=[pl.BlockSpec(memory_space=pltpu.SMEM)] + vmem(4),
        out_specs=vmem(1)[0],
        name="pack",
    )(
        token_pos,
        jnp.transpose(scale_exp, (1, 2, 0)).reshape(2, PAGES),
        page_owner.reshape(1, PAGES),
        prefill_keys.reshape(TOK, WIDTH),
        prefill_values.reshape(TOK, WIDTH),
    )
    tree = jnp.concatenate(
        [draft_keys.reshape(HALF, 2 * WIDTH), draft_values.reshape(HALF, 2 * WIDTH)], axis=1
    )
    xs = [shift(own, "x", 1), shift(own, "x", -1), shift(own, "x", 2)]
    far = shift(tree, "side", 1)
    near_x = jnp.concatenate(xs, axis=0)
    own_call = pl.pallas_call(
        own_kernel,
        out_shape=STATE,
        in_specs=vmem(6),
        out_specs=vmem(8),
        scratch_shapes=[pltpu.VMEM((TOK, WIDTH), BF), pltpu.VMEM((TOK, 2 * WIDTH), BF)],
        cost_estimate=cost(2),
        compiler_params=GRANT,
        name="own",
    )
    state = own_call(*(held(a) for a in (q, own, dq, tree, far)), parents.reshape(1, TOK))
    dxs = (-1, 1, 2)
    state = step(q, own, dq, [near_x], [[(0, d) for d in dxs]], state)
    ra = la = own
    rb = lb = near_x
    for s in range(1, 4):
        ra, la = shift(ra, "z", 1), shift(la, "z", -1)
        rb, lb = shift(rb, "z", 1), shift(lb, "z", -1)
        state = step(
            q, own, dq, [ra, la, rb, lb],
            [[(-s, 0)], [(s, 0)], [(-s, d) for d in dxs], [(s, d) for d in dxs]],
            state,
        )
    oa = shift(la, "z", -1)
    ob = shift(rb[: 2 * PAY], "z", 1)
    oc = shift(lb[2 * PAY :], "z", -1)
    out, ver, ck, cv = step(
        q, own, dq, [oa, ob, oc],
        [[(4, 0)], [(4, d) for d in dxs[:2]], [(4, dxs[2])]],
        state, last=True,
    )[8:]
    return (
        out.reshape(TOK, GROUPS, WIDTH),
        ck.reshape(TOK, 1, WIDTH),
        cv.reshape(TOK, 1, WIDTH),
        ver.reshape(8, GROUPS, WIDTH),
    )


def solution(mesh):
    finer = Mesh(
        mesh.devices.reshape(8, 4, mesh.shape["head"], mesh.shape["side"]),
        ("z", "x", "head", "side"),
    )
    full = P(CTX, ("head", "side"), None)
    in_specs = (
        full, full, full, P(CTX), full, P(CTX),
        P(None, ("head", "side"), None),
        P("side", "head", None), P("side", "head", None), P(),
    )
    return jax.shard_map(
        work, mesh=finer, in_specs=in_specs, out_specs=(full, full, full, full), check_vma=False
    )
```

```python
import functools

import jax
import jax.numpy as jnp
from jax import lax
from jax.experimental import pallas as pl
from jax.experimental.pallas import tpu as pltpu
from jax.sharding import Mesh
from jax.sharding import PartitionSpec as P


CTX = ("z", "x")
NEG = -1.0e30
LOG_TWO_E = 1.4426950408889634
TOK = 256
HALF = 128
GROUPS = 8
WIDTH = 128
PAGES = 32
EXTRA = 16
PAY = 2 * TOK + EXTRA
DEEP = WIDTH + EXTRA
QH = HALF * GROUPS
SLOTS = 4
PART = 256
COEF = WIDTH**-0.5 * LOG_TWO_E
BF = jnp.bfloat16
F32 = jnp.float32


def iota(shape, dim):
    return lax.broadcasted_iota(jnp.int32, shape, dim)


def dot_t(a, b):
    return lax.dot_general(a, b, (((1,), (1,)), ((), ())), preferred_element_type=F32)


def dot(a, b):
    return jnp.dot(a, b, preferred_element_type=F32)


def outside(x):
    return pltpu.with_memory_space_constraint(x, pltpu.HBM)


def held(x):
    return pltpu.with_memory_space_constraint(x, pltpu.VMEM)


def vmem(n):
    return [pl.BlockSpec(memory_space=pltpu.VMEM)] * n


def pack_kernel(
    pos_hbm, scale_hbm, owner_hbm, k_hbm, v_hbm, out_ref, pos_ref, scale_ref, owner_ref, v_ref, sems
):
    copies = [
        pltpu.make_async_copy(a, b, sems.at[i])
        for i, (a, b) in enumerate(
            (
                (v_hbm, v_ref),
                (k_hbm, out_ref.at[0:TOK, :]),
                (pos_hbm, pos_ref),
                (scale_hbm, scale_ref),
                (owner_hbm, owner_ref),
            )
        )
    ]
    for c in copies:
        c.start()
    for c in copies:
        c.wait()
    v = jnp.transpose(v_ref[...].astype(F32)).astype(BF)
    out_ref[TOK : TOK + HALF, :] = v[:, :HALF]
    out_ref[TOK + HALF : 2 * TOK, :] = v[:, HALF:]
    first = (pos_ref[0] // HALF).astype(F32)
    scale = scale_ref[...]
    bound = jnp.where(scale == -7, 3.5, jnp.where(scale == -6, 7.0, 14.0)).astype(F32)
    own = owner_ref[...].astype(F32)
    grow = (iota((PAGES, TOK), 0) == iota((PAGES, TOK), 1) // 8).astype(F32).astype(BF)
    row = iota((EXTRA, PAGES), 0)
    few = jnp.where(row < 2, bound[0:1, :], jnp.where(row < 4, bound[1:2, :], own))
    wide = dot(few.astype(BF), grow)
    row = iota((EXTRA, HALF), 0)
    left = (row == 0) | (row == 2) | (row == 4)
    meta = jnp.where(row < 6, jnp.where(left, wide[:, :HALF], wide[:, HALF:]), first)
    out_ref[2 * TOK :, :] = meta.astype(BF)


def me_index():
    return lax.axis_index("z") * 4 + lax.axis_index("x")


def weights_of(s, old):
    top = jnp.ceil(jnp.max(s, axis=0, keepdims=True))
    new = top if old is None else jnp.maximum(old, top)
    return new, jnp.exp2(s - new).astype(BF)


def verify_update(s, v_t, m_ref, l_ref, acc_ref, start=False):
    rows, keys = s.shape
    new = jnp.broadcast_to(jnp.ceil(jnp.max(s, axis=1, keepdims=True)), (rows, WIDTH))
    if not start:
        old = m_ref[...]
        new = jnp.maximum(old, new)
    p = jnp.exp2(s - jnp.tile(new, (1, keys // WIDTH)))
    mass = jnp.broadcast_to(jnp.sum(p, axis=1, keepdims=True), (rows, WIDTH))
    numer = dot_t(p.astype(BF), v_t)
    if not start:
        factor = jnp.exp2(old - new)
        mass = mass + l_ref[...] * factor
        numer = numer + acc_ref[...] * factor
    m_ref[...] = new
    l_ref[...] = mass
    acc_ref[...] = numer


def clipped_source(src_ref, base, col, mine, kc_ref, vc_ref, slot, ck_ref, cv_ref, b_ref):
    wide = src_ref[base + 2 * TOK : base + PAY, :].astype(F32)
    limit = slot * PAGES
    near = iota((PAGES // 2, HALF), 1) == 8 * iota((PAGES // 2, HALF), 0)
    picks = [jnp.where(near, wide[h : h + 1, :], 0.0) for h in range(2)]
    b_ref[limit : limit + PAGES, :] = dot(
        jnp.concatenate(picks, axis=0).astype(BF), jnp.ones((HALF, WIDTH), BF)
    )
    place = iota((2, HALF), 1) // 8 + 16 * iota((2, HALF), 0)
    hit = wide[4:6, :] == mine.astype(F32)
    page = jnp.max(jnp.where(hit, place, 0).astype(F32)).astype(jnp.int32)
    at = pl.ds(pl.multiple_of(col * 8, 8), 8)
    x = src_ref[base : base + TOK, :].astype(F32)
    pieces = []
    for p in range(PAGES):
        row = b_ref[pl.ds(limit + p, 8, stride=0), :]
        pieces.append(jnp.maximum(jnp.minimum(x[p * 8 : p * 8 + 8, :], row), -row))
    kc_ref[slot * TOK : (slot + 1) * TOK, :] = jnp.concatenate(pieces, axis=0).astype(BF)
    top = b_ref[pl.ds(limit + page, 8, stride=0), :]
    got = src_ref[pl.ds(pl.multiple_of(base + page * 8, 8), 8), :].astype(F32)
    ck_ref[at, :] = jnp.maximum(jnp.minimum(got, top), -top)
    total = None
    for h in range(2):
        raw = base + TOK + h * HALF
        row = wide[2 + h : 3 + h, :]
        x = src_ref[raw : raw + HALF, :].astype(F32)
        x = jnp.maximum(jnp.minimum(x, row), -row).astype(BF)
        vc_ref[2 * slot + h] = x
        one = iota((8, HALF), 1) + h * HALF == page * 8 + iota((8, HALF), 0)
        part = dot_t(one.astype(F32).astype(BF), x)
        total = part if total is None else total + part
    cv_ref[at, :] = total


def first_of(src_ref, base):
    meta = src_ref[base + 2 * TOK : base + PAY, :].astype(F32)
    return jnp.max(meta[8:, :]).astype(jnp.int32)


def joined(ref, first, count):
    return jnp.concatenate([ref[first + i] for i in range(count)], axis=1)


def own_kernel(
    q_ref, own_ref, dq_ref, tree_ref, far_ref, par_ref,
    m_ref, acc_ref, mv_ref, lv_ref, av_ref, ck_ref, cv_ref,
    kc_ref, vc_ref, b_ref,
):
    me = me_index()
    side = lax.axis_index("side")
    first = first_of(own_ref, 0)
    swap = (first >= PAGES).astype(jnp.int32)
    lo = pl.multiple_of(swap * HALF, HALF)
    hi = pl.multiple_of(HALF - swap * HALF, HALF)
    ones = jnp.ones((EXTRA, HALF), BF)
    k_lo, k_hi = own_ref[pl.ds(lo, HALF), :], own_ref[pl.ds(hi, HALF), :]
    v_lo = own_ref[pl.ds(pl.multiple_of(TOK + lo, HALF), HALF), :]
    v_hi = own_ref[pl.ds(pl.multiple_of(TOK + hi, HALF), HALF), :]
    v_lo = jnp.concatenate([v_lo, ones], axis=0)
    v_hi = jnp.concatenate([v_hi, ones], axis=0)
    k_both = jnp.concatenate([k_lo, k_hi], axis=0)
    v_both = jnp.concatenate([v_lo, v_hi], axis=1)
    for t in range(QH // PART):
        cols = slice(t * PART, (t + 1) * PART)
        token = iota((HALF, PART), 1) // GROUPS + t * PART // GROUPS
        open_ = iota((HALF, PART), 0) <= token
        q = q_ref[pl.ds(pl.multiple_of(hi * GROUPS + t * PART, PART), PART), :]
        s = dot_t(k_both, q) * COEF
        s = jnp.concatenate([s[:HALF], jnp.where(open_, s[HALF:], NEG)], axis=0)
        new, p = weights_of(s, None)
        acc_ref[1, :, cols] = dot(v_both, p)
        m_ref[1, :, cols] = jnp.broadcast_to(new, (8, PART))
        q = q_ref[pl.ds(pl.multiple_of(lo * GROUPS + t * PART, PART), PART), :]
        new, p = weights_of(jnp.where(open_, dot_t(k_lo, q) * COEF, NEG), None)
        acc_ref[0, :, cols] = dot(v_lo, p)
        m_ref[0, :, cols] = jnp.broadcast_to(new, (8, PART))

    link = (par_ref[...] == iota((TOK, TOK), 0)) | (iota((TOK, TOK), 0) == iota((TOK, TOK), 1))
    link = link.astype(F32).astype(BF)
    for _ in range(8):
        link = jnp.minimum(dot(link, link), 1.0).astype(BF)
    rows64 = GROUPS * 8
    take = iota((rows64, TOK), 1) == me * 8 + iota((rows64, TOK), 0) // GROUPS
    allowed = dot_t(take.astype(F32).astype(BF), link) > 0.5

    def head(ref, at):
        zero, one = ref[:, at : at + WIDTH], ref[:, at + WIDTH : at + 2 * WIDTH]
        return jnp.where(side == 0, zero, one)

    def rows_of(at):
        near, far = head(tree_ref, at), head(far_ref, at)
        return jnp.concatenate(
            [jnp.where(side == 0, near, far), jnp.where(side == 0, far, near)], axis=0
        )

    dq = dq_ref[pl.ds(pl.multiple_of(me * rows64, rows64), rows64), :]
    s = jnp.where(allowed, dot_t(dq, rows_of(0)) * COEF, NEG)
    v_t = jnp.transpose(rows_of(2 * WIDTH).astype(F32)).astype(BF)
    verify_update(s, v_t, mv_ref, lv_ref, av_ref, start=True)
    clipped_source(own_ref, 0, me, me, kc_ref, vc_ref, 0, ck_ref, cv_ref, b_ref)
    verify_update(dot_t(dq, kc_ref[...]) * COEF, joined(vc_ref, 0, 2), mv_ref, lv_ref, av_ref)


def flash_chunks(q_ref, q_at, half, k_ref, v_ref, base, chunks, m_ref, acc_ref):
    span = SLOTS * HALF

    def chunk(i, _):
        slot = base + i * SLOTS
        k = k_ref[pl.ds(pl.multiple_of(slot * HALF, HALF), span), :]
        v = joined(v_ref, slot, SLOTS)

        def scores(t):
            q = q_ref[pl.ds(pl.multiple_of(q_at + t * PART, PART), PART), :]
            return dot_t(k, q) * COEF

        s = scores(0)
        for t in range(QH // PART):
            ahead = scores(t + 1) if t + 1 < QH // PART else None
            cols = slice(t * PART, (t + 1) * PART)
            old = m_ref[half, 0:1, cols]
            new, p = weights_of(s, old)
            acc_ref[half, :, cols] = acc_ref[half, :, cols] * jnp.exp2(old - new) + dot(v, p)
            m_ref[half, :, cols] = jnp.broadcast_to(new, (8, PART))
            s = ahead
        return 0

    lax.fori_loop(0, chunks, chunk, 0)


def step_kernel(layout, last, *refs):
    n_in = len(layout)
    q_ref, own_ref, dq_ref = refs[:3]
    srcs = refs[3 : 3 + n_in]
    state = refs[3 + n_in + len(STATE) : 3 + n_in + 2 * len(STATE)]
    if last:
        out_ref, ver_ref, ok_ref, ov_ref = refs[3 + n_in + 2 * len(STATE) :][:4]
    kk_ref, vv_ref, kc_ref, vc_ref, b_ref = refs[-5:]
    m_ref, acc_ref, mv_ref, lv_ref, av_ref, ck_ref, cv_ref = state
    me, z, x = me_index(), lax.axis_index("z"), lax.axis_index("x")
    first = first_of(own_ref, 0)
    swap = (first >= PAGES).astype(jnp.int32)
    mine = jnp.minimum(first, 2 * PAGES - 1 - first)
    blocks = [(r, i * PAY, d) for r, ds in zip(srcs, layout) for i, d in enumerate(ds)]
    n = len(blocks)
    lo_base = 2 * n + SLOTS
    ones = jnp.ones((EXTRA, HALF), BF)
    n_hi, n_lo = jnp.int32(0), jnp.int32(0)
    for i, (ref, base, _) in enumerate(blocks):
        f = first_of(ref, base)
        other = (f >= PAGES).astype(jnp.int32)
        later = (jnp.minimum(f, 2 * PAGES - 1 - f) > mine).astype(jnp.int32)
        lo = base + other * HALF
        hi = base + HALF - other * HALF
        sel = jnp.where(later == 1, hi, lo)
        to = jnp.where(later == 1, n + n_hi, lo_base + n_lo)
        kk_ref[i * HALF : (i + 1) * HALF, :] = ref[pl.ds(pl.multiple_of(lo, 16), HALF), :]
        vv_ref[i, :WIDTH, :] = ref[pl.ds(pl.multiple_of(lo + TOK, 16), HALF), :]
        vv_ref[i, WIDTH:, :] = ones
        at = pl.ds(pl.multiple_of(to * HALF, HALF), HALF)
        kk_ref[at, :] = ref[pl.ds(pl.multiple_of(sel, 16), HALF), :]
        vv_ref[to, :WIDTH, :] = ref[pl.ds(pl.multiple_of(sel + TOK, 16), HALF), :]
        vv_ref[to, WIDTH:, :] = ones
        n_hi, n_lo = n_hi + later, n_lo + 1 - later
    for start, count in ((0, n + n_hi), (lo_base, n_lo)):
        for j in range(SLOTS - 1):
            at = pl.ds(pl.multiple_of((start + count + j) * HALF, HALF), HALF)
            kk_ref[at, :] = kk_ref[start * HALF : (start + 1) * HALF, :]
            vv_ref[start + count + j] = jnp.zeros((DEEP, HALF), BF)
    q_lo = swap * QH
    q_hi = QH - swap * QH
    ways = ((q_hi, 1, 0, n + n_hi), (q_lo, 0, lo_base, n_lo))
    for q_at, half, base, count in ways:
        chunks = (count + SLOTS - 1) // SLOTS
        flash_chunks(q_ref, q_at, half, kk_ref, vv_ref, base, chunks, m_ref, acc_ref)

    for i, (ref, base, (dz, dx)) in enumerate(blocks):
        col = ((z + dz + 8) % 8) * 4 + (x + dx + 4) % 4
        clipped_source(ref, base, col, me, kc_ref, vc_ref, i, ck_ref, cv_ref, b_ref)
    rows64 = GROUPS * 8
    dq = dq_ref[pl.ds(pl.multiple_of(me * rows64, rows64), rows64), :]
    verify_update(dot_t(dq, kc_ref[...]) * COEF, joined(vc_ref, 0, 2 * n), mv_ref, lv_ref, av_ref)
    if last:
        for t in range(QH // PART):
            cols = slice(t * PART, (t + 1) * PART)
            for at, half in ((q_hi, 1), (q_lo, 0)):
                a = acc_ref[half, :, cols]
                out = jnp.transpose(a[:WIDTH] / a[WIDTH : WIDTH + 1])
                out_ref[pl.ds(pl.multiple_of(at + t * PART, PART), PART), :] = out.astype(BF)
        ver_ref[...] = (av_ref[...] / lv_ref[...]).astype(BF)
        ok_ref[...] = ck_ref[...].astype(BF)
        ov_ref[...] = cv_ref[...].astype(BF)


STATE = [
    pltpu.VMEM((2, 8, QH), F32),
    pltpu.VMEM((2, DEEP, QH), F32),
    pltpu.VMEM((64, WIDTH), F32),
    pltpu.VMEM((64, WIDTH), F32),
    pltpu.VMEM((64, WIDTH), F32),
    pltpu.VMEM((TOK, WIDTH), F32),
    pltpu.VMEM((TOK, WIDTH), F32),
]
GRANT = pltpu.CompilerParams(vmem_limit_bytes=40 * 1024 * 1024)


def cost(n):
    return pl.CostEstimate(
        flops=n * 4 * TOK * QH * WIDTH, bytes_accessed=n * PAY * WIDTH * 2, transcendentals=0
    )


def step(q, own, dq, sources, layout, state, last=False):
    n = sum(len(d) for d in layout)
    outs = STATE
    alias = {3 + len(layout) + i: i for i in range(len(STATE))}
    if last:
        outs = STATE + [
            jax.ShapeDtypeStruct((2 * QH, WIDTH), BF),
            jax.ShapeDtypeStruct((64, WIDTH), BF),
            jax.ShapeDtypeStruct((TOK, WIDTH), BF),
            jax.ShapeDtypeStruct((TOK, WIDTH), BF),
        ]
    slots = 3 * n + 2 * SLOTS
    return pl.pallas_call(
        functools.partial(step_kernel, layout, last),
        out_shape=outs,
        in_specs=vmem(3 + len(layout) + len(STATE)),
        out_specs=vmem(len(outs)),
        scratch_shapes=[
            pltpu.VMEM((slots * HALF, WIDTH), BF),
            pltpu.VMEM((slots, DEEP, HALF), BF),
            pltpu.VMEM((n * TOK, WIDTH), BF),
            pltpu.VMEM((2 * n, HALF, WIDTH), BF),
            pltpu.VMEM((n * PAGES, WIDTH), F32),
        ],
        input_output_aliases=alias,
        cost_estimate=cost(n),
        compiler_params=GRANT,
    )(*(held(a) for a in (q, own, dq, *sources, *state)))


def shift(b, axis, d):
    n = lax.axis_size(axis)
    return lax.ppermute(b, axis, [(i, (i + d) % n) for i in range(n)])


def work(
    prefill_query, prefill_keys, prefill_values, token_pos, scale_exp, page_owner,
    draft_query, draft_keys, draft_values, parents,
):
    q = prefill_query.reshape(2 * QH, WIDTH)
    dq = draft_query.reshape(2 * QH, WIDTH)
    own = pl.pallas_call(
        pack_kernel,
        out_shape=pltpu.VMEM((PAY, WIDTH), BF),
        compiler_params=pltpu.CompilerParams(vmem_limit_bytes=4 * 1024 * 1024),
        in_specs=[pl.BlockSpec(memory_space=pl.ANY)] * 5,
        out_specs=vmem(1)[0],
        scratch_shapes=[
            pltpu.SMEM((TOK,), jnp.int32),
            pltpu.VMEM((2, PAGES), jnp.int32),
            pltpu.VMEM((1, PAGES), jnp.int32),
            pltpu.VMEM((TOK, WIDTH), BF),
            pltpu.SemaphoreType.DMA((5,)),
        ],
        name="pack",
    )(
        outside(token_pos),
        outside(jnp.transpose(scale_exp, (1, 2, 0)).reshape(2, PAGES)),
        outside(page_owner.reshape(1, PAGES)),
        outside(prefill_keys.reshape(TOK, WIDTH)),
        outside(prefill_values.reshape(TOK, WIDTH)),
    )
    tree = jnp.concatenate(
        [draft_keys.reshape(HALF, 2 * WIDTH), draft_values.reshape(HALF, 2 * WIDTH)], axis=1
    )
    xs = [shift(own, "x", 1), shift(own, "x", -1), shift(own, "x", 2)]
    far = shift(tree, "side", 1)
    near_x = jnp.concatenate(xs, axis=0)
    own_call = pl.pallas_call(
        own_kernel,
        out_shape=STATE,
        in_specs=vmem(6),
        out_specs=vmem(len(STATE)),
        scratch_shapes=[
            pltpu.VMEM((TOK, WIDTH), BF),
            pltpu.VMEM((2, HALF, WIDTH), BF),
            pltpu.VMEM((PAGES, WIDTH), F32),
        ],
        cost_estimate=cost(2),
        compiler_params=GRANT,
        name="own",
    )
    state = own_call(*(held(a) for a in (q, own, dq, tree, far)), parents.reshape(1, TOK))
    dxs = (-1, 1, 2)
    state = step(q, own, dq, [near_x], [[(0, d) for d in dxs]], state)
    ra = la = own
    rb = lb = near_x
    for s in range(1, 4):
        ra, la = shift(ra, "z", 1), shift(la, "z", -1)
        rb, lb = shift(rb, "z", 1), shift(lb, "z", -1)
        state = step(
            q, own, dq, [ra, la, rb, lb],
            [[(-s, 0)], [(s, 0)], [(-s, d) for d in dxs], [(s, d) for d in dxs]],
            state,
        )
    oa = shift(la, "z", -1)
    ob = shift(rb[: 2 * PAY], "z", 1)
    oc = shift(lb[2 * PAY :], "z", -1)
    out, ver, ck, cv = step(
        q, own, dq, [oa, ob, oc],
        [[(4, 0)], [(4, d) for d in dxs[:2]], [(4, dxs[2])]],
        state, last=True,
    )[len(STATE) :]
    return (
        out.reshape(TOK, GROUPS, WIDTH),
        ck.reshape(TOK, 1, WIDTH),
        cv.reshape(TOK, 1, WIDTH),
        ver.reshape(8, GROUPS, WIDTH),
    )


def solution(mesh):
    finer = Mesh(
        mesh.devices.reshape(8, 4, mesh.shape["head"], mesh.shape["side"]),
        ("z", "x", "head", "side"),
    )
    full = P(CTX, ("head", "side"), None)
    in_specs = (
        full, full, full, P(CTX), full, P(CTX),
        P(None, ("head", "side"), None),
        P("side", "head", None), P("side", "head", None), P(),
    )
    return jax.shard_map(
        work, mesh=finer, in_specs=in_specs, out_specs=(full, full, full, full), check_vma=False
    )
```

```python
import functools

import jax
import jax.numpy as jnp
from jax import lax
from jax.experimental import pallas as pl
from jax.experimental.pallas import tpu as pltpu
from jax.sharding import Mesh
from jax.sharding import PartitionSpec as P


CTX = ("z", "x")
NEG = -1.0e30
LOG_TWO_E = 1.4426950408889634
TOK = 256
HALF = 128
GROUPS = 8
WIDTH = 128
PAGES = 32
EXTRA = 16
PAY = 2 * TOK + EXTRA
DEEP = WIDTH + EXTRA
QH = HALF * GROUPS
SLOTS = 4
PART = 512
COEF = WIDTH**-0.5 * LOG_TWO_E
BF = jnp.bfloat16
F32 = jnp.float32


def iota(shape, dim):
    return lax.broadcasted_iota(jnp.int32, shape, dim)


def dot_t(a, b):
    return lax.dot_general(a, b, (((1,), (1,)), ((), ())), preferred_element_type=F32)


def dot(a, b):
    return jnp.dot(a, b, preferred_element_type=F32)


def outside(x):
    return pltpu.with_memory_space_constraint(x, pltpu.HBM)


def held(x):
    return pltpu.with_memory_space_constraint(x, pltpu.VMEM)


def vmem(n):
    return [pl.BlockSpec(memory_space=pltpu.VMEM)] * n


def pack_kernel(
    pos_hbm, scale_hbm, owner_hbm, k_hbm, v_hbm, out_ref, pos_ref, scale_ref, owner_ref, v_ref, sems
):
    copies = [
        pltpu.make_async_copy(a, b, sems.at[i])
        for i, (a, b) in enumerate(
            (
                (v_hbm, v_ref),
                (k_hbm, out_ref.at[0:TOK, :]),
                (pos_hbm, pos_ref),
                (scale_hbm, scale_ref),
                (owner_hbm, owner_ref),
            )
        )
    ]
    for c in copies:
        c.start()
    for c in copies:
        c.wait()
    v = jnp.transpose(v_ref[...].astype(F32)).astype(BF)
    out_ref[TOK : TOK + HALF, :] = v[:, :HALF]
    out_ref[TOK + HALF : 2 * TOK, :] = v[:, HALF:]
    first = (pos_ref[0] // HALF).astype(F32)
    scale = scale_ref[...]
    bound = jnp.where(scale == -7, 3.5, jnp.where(scale == -6, 7.0, 14.0)).astype(F32)
    own = owner_ref[...].astype(F32)
    grow = (iota((PAGES, TOK), 0) == iota((PAGES, TOK), 1) // 8).astype(F32).astype(BF)
    row = iota((EXTRA, PAGES), 0)
    few = jnp.where(row < 2, bound[0:1, :], jnp.where(row < 4, bound[1:2, :], own))
    wide = dot(few.astype(BF), grow)
    row = iota((EXTRA, HALF), 0)
    left = (row == 0) | (row == 2) | (row == 4)
    meta = jnp.where(row < 6, jnp.where(left, wide[:, :HALF], wide[:, HALF:]), first)
    out_ref[2 * TOK :, :] = meta.astype(BF)


def me_index():
    return lax.axis_index("z") * 4 + lax.axis_index("x")


def weights_of(s, old):
    top = jnp.ceil(jnp.max(s, axis=0, keepdims=True) * COEF)
    new = top if old is None else jnp.maximum(old, top)
    return new, jnp.exp2(s * COEF - new).astype(BF)


def verify_update(s, v_t, m_ref, l_ref, acc_ref, start=False):
    rows, keys = s.shape
    new = jnp.broadcast_to(jnp.ceil(jnp.max(s, axis=1, keepdims=True)), (rows, WIDTH))
    if not start:
        old = m_ref[...]
        new = jnp.maximum(old, new)
    p = jnp.exp2(s - jnp.tile(new, (1, keys // WIDTH)))
    mass = jnp.broadcast_to(jnp.sum(p, axis=1, keepdims=True), (rows, WIDTH))
    numer = dot_t(p.astype(BF), v_t)
    if not start:
        factor = jnp.exp2(old - new)
        mass = mass + l_ref[...] * factor
        numer = numer + acc_ref[...] * factor
    m_ref[...] = new
    l_ref[...] = mass
    acc_ref[...] = numer


def clipped_source(src_ref, base, col, mine, kc_ref, vc_ref, slot, ck_ref, cv_ref, b_ref):
    wide = src_ref[base + 2 * TOK : base + PAY, :].astype(F32)
    limit = slot * PAGES
    near = iota((PAGES // 2, HALF), 1) == 8 * iota((PAGES // 2, HALF), 0)
    picks = [jnp.where(near, wide[h : h + 1, :], 0.0) for h in range(2)]
    b_ref[limit : limit + PAGES, :] = dot(
        jnp.concatenate(picks, axis=0).astype(BF), jnp.ones((HALF, WIDTH), BF)
    )
    place = iota((2, HALF), 1) // 8 + 16 * iota((2, HALF), 0)
    hit = wide[4:6, :] == mine.astype(F32)
    page = jnp.max(jnp.where(hit, place, 0).astype(F32)).astype(jnp.int32)
    at = pl.ds(pl.multiple_of(col * 8, 8), 8)
    x = src_ref[base : base + TOK, :].astype(F32)
    pieces = []
    for p in range(PAGES):
        row = b_ref[pl.ds(limit + p, 8, stride=0), :]
        pieces.append(jnp.maximum(jnp.minimum(x[p * 8 : p * 8 + 8, :], row), -row))
    kc_ref[slot * TOK : (slot + 1) * TOK, :] = jnp.concatenate(pieces, axis=0).astype(BF)
    top = b_ref[pl.ds(limit + page, 8, stride=0), :]
    got = src_ref[pl.ds(pl.multiple_of(base + page * 8, 8), 8), :].astype(F32)
    ck_ref[at, :] = jnp.maximum(jnp.minimum(got, top), -top)
    total = None
    for h in range(2):
        raw = base + TOK + h * HALF
        row = wide[2 + h : 3 + h, :]
        x = src_ref[raw : raw + HALF, :].astype(F32)
        x = jnp.maximum(jnp.minimum(x, row), -row).astype(BF)
        vc_ref[2 * slot + h] = x
        one = iota((8, HALF), 1) + h * HALF == page * 8 + iota((8, HALF), 0)
        part = dot_t(one.astype(F32).astype(BF), x)
        total = part if total is None else total + part
    cv_ref[at, :] = total


def first_of(src_ref, base):
    meta = src_ref[base + 2 * TOK : base + PAY, :].astype(F32)
    return jnp.max(meta[8:, :]).astype(jnp.int32)


def joined(ref, first, count):
    return jnp.concatenate([ref[first + i] for i in range(count)], axis=1)


def own_kernel(
    q_ref, own_ref, dq_ref, tree_ref, far_ref, par_ref,
    m_ref, acc_ref, mv_ref, lv_ref, av_ref, ck_ref, cv_ref,
    kc_ref, vc_ref, b_ref,
):
    me = me_index()
    side = lax.axis_index("side")
    first = first_of(own_ref, 0)
    swap = (first >= PAGES).astype(jnp.int32)
    lo = pl.multiple_of(swap * HALF, HALF)
    hi = pl.multiple_of(HALF - swap * HALF, HALF)
    ones = jnp.ones((EXTRA, HALF), BF)
    k_lo, k_hi = own_ref[pl.ds(lo, HALF), :], own_ref[pl.ds(hi, HALF), :]
    v_lo = own_ref[pl.ds(pl.multiple_of(TOK + lo, HALF), HALF), :]
    v_hi = own_ref[pl.ds(pl.multiple_of(TOK + hi, HALF), HALF), :]
    v_lo = jnp.concatenate([v_lo, ones], axis=0)
    v_hi = jnp.concatenate([v_hi, ones], axis=0)
    k_both = jnp.concatenate([k_lo, k_hi], axis=0)
    v_both = jnp.concatenate([v_lo, v_hi], axis=1)
    for t in range(QH // PART):
        cols = slice(t * PART, (t + 1) * PART)
        token = iota((HALF, PART), 1) // GROUPS + t * PART // GROUPS
        open_ = iota((HALF, PART), 0) <= token
        q = q_ref[pl.ds(pl.multiple_of(hi * GROUPS + t * PART, PART), PART), :]
        s = dot_t(k_both, q)
        s = jnp.concatenate([s[:HALF], jnp.where(open_, s[HALF:], NEG)], axis=0)
        new, p = weights_of(s, None)
        acc_ref[1, :, cols] = dot(v_both, p)
        m_ref[1, :, cols] = jnp.broadcast_to(new, (8, PART))
        q = q_ref[pl.ds(pl.multiple_of(lo * GROUPS + t * PART, PART), PART), :]
        new, p = weights_of(jnp.where(open_, dot_t(k_lo, q), NEG), None)
        acc_ref[0, :, cols] = dot(v_lo, p)
        m_ref[0, :, cols] = jnp.broadcast_to(new, (8, PART))

    link = (par_ref[...] == iota((TOK, TOK), 0)) | (iota((TOK, TOK), 0) == iota((TOK, TOK), 1))
    link = link.astype(F32).astype(BF)
    for _ in range(8):
        link = jnp.minimum(dot(link, link), 1.0).astype(BF)
    rows64 = GROUPS * 8
    take = iota((rows64, TOK), 1) == me * 8 + iota((rows64, TOK), 0) // GROUPS
    allowed = dot_t(take.astype(F32).astype(BF), link) > 0.5

    def head(ref, at):
        zero, one = ref[:, at : at + WIDTH], ref[:, at + WIDTH : at + 2 * WIDTH]
        return jnp.where(side == 0, zero, one)

    def rows_of(at):
        near, far = head(tree_ref, at), head(far_ref, at)
        return jnp.concatenate(
            [jnp.where(side == 0, near, far), jnp.where(side == 0, far, near)], axis=0
        )

    dq = dq_ref[pl.ds(pl.multiple_of(me * rows64, rows64), rows64), :]
    s = jnp.where(allowed, dot_t(dq, rows_of(0)) * COEF, NEG)
    v_t = jnp.transpose(rows_of(2 * WIDTH).astype(F32)).astype(BF)
    verify_update(s, v_t, mv_ref, lv_ref, av_ref, start=True)
    clipped_source(own_ref, 0, me, me, kc_ref, vc_ref, 0, ck_ref, cv_ref, b_ref)
    verify_update(dot_t(dq, kc_ref[...]) * COEF, joined(vc_ref, 0, 2), mv_ref, lv_ref, av_ref)


def flash_chunks(q_ref, q_at, half, k_ref, v_ref, base, count, m_ref, acc_ref, s_ref):
    def chunk(slot, slots):
        span = slots * HALF
        k = k_ref[pl.ds(pl.multiple_of(slot * HALF, HALF), span), :]
        v = joined(v_ref, slot, slots)
        tiles = range(QH // PART)
        tops = []
        for t in tiles:
            q = q_ref[pl.ds(pl.multiple_of(q_at + t * PART, PART), PART), :]
            s = dot_t(k, q)
            s_ref[t, :span] = s
            tops.append(jnp.ceil(jnp.max(s, axis=0, keepdims=True) * COEF))
        for t in tiles:
            cols = slice(t * PART, (t + 1) * PART)
            old = m_ref[half, 0:1, cols]
            new = jnp.maximum(old, tops[t])
            p = jnp.exp2(s_ref[t, :span] * COEF - new).astype(BF)
            acc_ref[half, :, cols] = acc_ref[half, :, cols] * jnp.exp2(old - new) + dot(v, p)
            m_ref[half, :, cols] = jnp.broadcast_to(new, (8, PART))

    def full(i, _):
        chunk(base + i * SLOTS, SLOTS)
        return 0

    many = (count + 1) // SLOTS
    lax.fori_loop(0, many, full, 0)

    @pl.when(count > many * SLOTS)
    def _():
        chunk(base + many * SLOTS, SLOTS // 2)


def step_kernel(layout, last, *refs):
    n_in = len(layout)
    q_ref, own_ref, dq_ref = refs[:3]
    srcs = refs[3 : 3 + n_in]
    state = refs[3 + n_in + len(STATE) : 3 + n_in + 2 * len(STATE)]
    if last:
        out_ref, ver_ref, ok_ref, ov_ref = refs[3 + n_in + 2 * len(STATE) :][:4]
    kk_ref, vv_ref, kc_ref, vc_ref, b_ref, s_ref = refs[-6:]
    m_ref, acc_ref, mv_ref, lv_ref, av_ref, ck_ref, cv_ref = state
    me, z, x = me_index(), lax.axis_index("z"), lax.axis_index("x")
    first = first_of(own_ref, 0)
    swap = (first >= PAGES).astype(jnp.int32)
    mine = jnp.minimum(first, 2 * PAGES - 1 - first)
    blocks = [(r, i * PAY, d) for r, ds in zip(srcs, layout) for i, d in enumerate(ds)]
    n = len(blocks)
    lo_base = 2 * n + SLOTS
    ones = jnp.ones((EXTRA, HALF), BF)
    n_hi, n_lo = jnp.int32(0), jnp.int32(0)
    for i, (ref, base, _) in enumerate(blocks):
        f = first_of(ref, base)
        other = (f >= PAGES).astype(jnp.int32)
        later = (jnp.minimum(f, 2 * PAGES - 1 - f) > mine).astype(jnp.int32)
        lo = base + other * HALF
        hi = base + HALF - other * HALF
        sel = jnp.where(later == 1, hi, lo)
        to = jnp.where(later == 1, n + n_hi, lo_base + n_lo)
        kk_ref[i * HALF : (i + 1) * HALF, :] = ref[pl.ds(pl.multiple_of(lo, 16), HALF), :]
        vv_ref[i, :WIDTH, :] = ref[pl.ds(pl.multiple_of(lo + TOK, 16), HALF), :]
        vv_ref[i, WIDTH:, :] = ones
        at = pl.ds(pl.multiple_of(to * HALF, HALF), HALF)
        kk_ref[at, :] = ref[pl.ds(pl.multiple_of(sel, 16), HALF), :]
        vv_ref[to, :WIDTH, :] = ref[pl.ds(pl.multiple_of(sel + TOK, 16), HALF), :]
        vv_ref[to, WIDTH:, :] = ones
        n_hi, n_lo = n_hi + later, n_lo + 1 - later
    for start, count in ((0, n + n_hi), (lo_base, n_lo)):
        for j in range(1):
            at = pl.ds(pl.multiple_of((start + count + j) * HALF, HALF), HALF)
            kk_ref[at, :] = kk_ref[start * HALF : (start + 1) * HALF, :]
            vv_ref[start + count + j] = jnp.zeros((DEEP, HALF), BF)
    q_lo = swap * QH
    q_hi = QH - swap * QH
    ways = ((q_hi, 1, 0, n + n_hi), (q_lo, 0, lo_base, n_lo))
    for q_at, half, base, count in ways:
        flash_chunks(q_ref, q_at, half, kk_ref, vv_ref, base, count, m_ref, acc_ref, s_ref)

    for i, (ref, base, (dz, dx)) in enumerate(blocks):
        col = ((z + dz + 8) % 8) * 4 + (x + dx + 4) % 4
        clipped_source(ref, base, col, me, kc_ref, vc_ref, i, ck_ref, cv_ref, b_ref)
    rows64 = GROUPS * 8
    dq = dq_ref[pl.ds(pl.multiple_of(me * rows64, rows64), rows64), :]
    verify_update(dot_t(dq, kc_ref[...]) * COEF, joined(vc_ref, 0, 2 * n), mv_ref, lv_ref, av_ref)
    if last:
        for t in range(QH // PART):
            cols = slice(t * PART, (t + 1) * PART)
            for at, half in ((q_hi, 1), (q_lo, 0)):
                a = acc_ref[half, :, cols]
                out = jnp.transpose(a[:WIDTH] / a[WIDTH : WIDTH + 1])
                out_ref[pl.ds(pl.multiple_of(at + t * PART, PART), PART), :] = out.astype(BF)
        ver_ref[...] = (av_ref[...] / lv_ref[...]).astype(BF)
        ok_ref[...] = ck_ref[...].astype(BF)
        ov_ref[...] = cv_ref[...].astype(BF)


STATE = [
    pltpu.VMEM((2, 8, QH), F32),
    pltpu.VMEM((2, DEEP, QH), F32),
    pltpu.VMEM((64, WIDTH), F32),
    pltpu.VMEM((64, WIDTH), F32),
    pltpu.VMEM((64, WIDTH), F32),
    pltpu.VMEM((TOK, WIDTH), F32),
    pltpu.VMEM((TOK, WIDTH), F32),
]
GRANT = pltpu.CompilerParams(vmem_limit_bytes=40 * 1024 * 1024)


def cost(n):
    return pl.CostEstimate(
        flops=n * 4 * TOK * QH * WIDTH, bytes_accessed=n * PAY * WIDTH * 2, transcendentals=0
    )


def step(q, own, dq, sources, layout, state, last=False):
    n = sum(len(d) for d in layout)
    outs = STATE
    alias = {3 + len(layout) + i: i for i in range(len(STATE))}
    if last:
        outs = STATE + [
            jax.ShapeDtypeStruct((2 * QH, WIDTH), BF),
            jax.ShapeDtypeStruct((64, WIDTH), BF),
            jax.ShapeDtypeStruct((TOK, WIDTH), BF),
            jax.ShapeDtypeStruct((TOK, WIDTH), BF),
        ]
    slots = 3 * n + 2 * SLOTS
    return pl.pallas_call(
        functools.partial(step_kernel, layout, last),
        out_shape=outs,
        in_specs=vmem(3 + len(layout) + len(STATE)),
        out_specs=vmem(len(outs)),
        scratch_shapes=[
            pltpu.VMEM((slots * HALF, WIDTH), BF),
            pltpu.VMEM((slots, DEEP, HALF), BF),
            pltpu.VMEM((n * TOK, WIDTH), BF),
            pltpu.VMEM((2 * n, HALF, WIDTH), BF),
            pltpu.VMEM((n * PAGES, WIDTH), F32),
            pltpu.VMEM((QH // PART, SLOTS * HALF, PART), F32),
        ],
        input_output_aliases=alias,
        cost_estimate=cost(n),
        compiler_params=GRANT,
    )(*(held(a) for a in (q, own, dq, *sources, *state)))


def shift(b, axis, d):
    n = lax.axis_size(axis)
    return lax.ppermute(b, axis, [(i, (i + d) % n) for i in range(n)])


def work(
    prefill_query, prefill_keys, prefill_values, token_pos, scale_exp, page_owner,
    draft_query, draft_keys, draft_values, parents,
):
    q = prefill_query.reshape(2 * QH, WIDTH)
    dq = draft_query.reshape(2 * QH, WIDTH)
    own = pl.pallas_call(
        pack_kernel,
        out_shape=pltpu.VMEM((PAY, WIDTH), BF),
        compiler_params=pltpu.CompilerParams(vmem_limit_bytes=4 * 1024 * 1024),
        in_specs=[pl.BlockSpec(memory_space=pl.ANY)] * 5,
        out_specs=vmem(1)[0],
        scratch_shapes=[
            pltpu.SMEM((TOK,), jnp.int32),
            pltpu.VMEM((2, PAGES), jnp.int32),
            pltpu.VMEM((1, PAGES), jnp.int32),
            pltpu.VMEM((TOK, WIDTH), BF),
            pltpu.SemaphoreType.DMA((5,)),
        ],
        name="pack",
    )(
        outside(token_pos),
        outside(jnp.transpose(scale_exp, (1, 2, 0)).reshape(2, PAGES)),
        outside(page_owner.reshape(1, PAGES)),
        outside(prefill_keys.reshape(TOK, WIDTH)),
        outside(prefill_values.reshape(TOK, WIDTH)),
    )
    tree = jnp.concatenate(
        [draft_keys.reshape(HALF, 2 * WIDTH), draft_values.reshape(HALF, 2 * WIDTH)], axis=1
    )
    xs = [shift(own, "x", 1), shift(own, "x", -1), shift(own, "x", 2)]
    far = shift(tree, "side", 1)
    near_x = jnp.concatenate(xs, axis=0)
    own_call = pl.pallas_call(
        own_kernel,
        out_shape=STATE,
        in_specs=vmem(6),
        out_specs=vmem(len(STATE)),
        scratch_shapes=[
            pltpu.VMEM((TOK, WIDTH), BF),
            pltpu.VMEM((2, HALF, WIDTH), BF),
            pltpu.VMEM((PAGES, WIDTH), F32),
        ],
        cost_estimate=cost(2),
        compiler_params=GRANT,
        name="own",
    )
    state = own_call(*(held(a) for a in (q, own, dq, tree, far, parents.reshape(1, TOK))))
    dxs = (-1, 1, 2)
    state = step(q, own, dq, [near_x], [[(0, d) for d in dxs]], state)
    ra = la = own
    rb = lb = near_x
    for s in range(1, 4):
        ra, la = shift(ra, "z", 1), shift(la, "z", -1)
        rb, lb = shift(rb, "z", 1), shift(lb, "z", -1)
        state = step(
            q, own, dq, [ra, la, rb, lb],
            [[(-s, 0)], [(s, 0)], [(-s, d) for d in dxs], [(s, d) for d in dxs]],
            state,
        )
    ob = shift(rb[: 2 * PAY], "z", 1)
    oc = shift(jnp.concatenate([la, lb[2 * PAY :]], axis=0), "z", -1)
    out, ver, ck, cv = step(
        q, own, dq, [ob, oc],
        [[(4, d) for d in dxs[:2]], [(4, 0), (4, dxs[2])]],
        state, last=True,
    )[len(STATE) :]
    return (
        out.reshape(TOK, GROUPS, WIDTH),
        ck.reshape(TOK, 1, WIDTH),
        cv.reshape(TOK, 1, WIDTH),
        ver.reshape(8, GROUPS, WIDTH),
    )


def solution(mesh):
    finer = Mesh(
        mesh.devices.reshape(8, 4, mesh.shape["head"], mesh.shape["side"]),
        ("z", "x", "head", "side"),
    )
    full = P(CTX, ("head", "side"), None)
    in_specs = (
        full, full, full, P(CTX), full, P(CTX),
        P(None, ("head", "side"), None),
        P("side", "head", None), P("side", "head", None), P(),
    )
    return jax.shard_map(
        work, mesh=finer, in_specs=in_specs, out_specs=(full, full, full, full), check_vma=False
    )
```

```python
import functools

import jax
import jax.numpy as jnp
from jax import lax
from jax.experimental import pallas as pl
from jax.experimental.pallas import tpu as pltpu
from jax.sharding import Mesh
from jax.sharding import PartitionSpec as P


CTX = ("z", "x")
NEG = -1.0e30
LOG_TWO_E = 1.4426950408889634
TOK = 256
HALF = 128
GROUPS = 8
WIDTH = 128
PAGES = 32
EXTRA = 16
PAY = 2 * TOK + EXTRA
DEEP = WIDTH + EXTRA
QH = HALF * GROUPS
SLOTS = 4
PART = 512
COEF = WIDTH**-0.5 * LOG_TWO_E
BF = jnp.bfloat16
F32 = jnp.float32


def iota(shape, dim):
    return lax.broadcasted_iota(jnp.int32, shape, dim)


def dot_t(a, b):
    return lax.dot_general(a, b, (((1,), (1,)), ((), ())), preferred_element_type=F32)


def dot(a, b):
    return jnp.dot(a, b, preferred_element_type=F32)


def outside(x):
    return pltpu.with_memory_space_constraint(x, pltpu.HBM)


def held(x):
    return pltpu.with_memory_space_constraint(x, pltpu.VMEM)


def vmem(n):
    return [pl.BlockSpec(memory_space=pltpu.VMEM)] * n


def pack_kernel(
    pos_hbm, scale_hbm, owner_hbm, k_hbm, v_hbm, out_ref, pos_ref, scale_ref, owner_ref, v_ref, sems
):
    copies = [
        pltpu.make_async_copy(a, b, sems.at[i])
        for i, (a, b) in enumerate(
            (
                (v_hbm, v_ref),
                (k_hbm, out_ref.at[0:TOK, :]),
                (pos_hbm, pos_ref),
                (scale_hbm, scale_ref),
                (owner_hbm, owner_ref),
            )
        )
    ]
    for c in copies:
        c.start()
    for c in copies:
        c.wait()
    v = jnp.transpose(v_ref[...].astype(F32)).astype(BF)
    out_ref[TOK : TOK + HALF, :] = v[:, :HALF]
    out_ref[TOK + HALF : 2 * TOK, :] = v[:, HALF:]
    first = (pos_ref[0] // HALF).astype(F32)
    scale = scale_ref[...]
    bound = jnp.where(scale == -7, 3.5, jnp.where(scale == -6, 7.0, 14.0)).astype(F32)
    own = owner_ref[...].astype(F32)
    grow = (iota((PAGES, TOK), 0) == iota((PAGES, TOK), 1) // 8).astype(F32).astype(BF)
    row = iota((EXTRA, PAGES), 0)
    few = jnp.where(row < 2, bound[0:1, :], jnp.where(row < 4, bound[1:2, :], own))
    wide = dot(few.astype(BF), grow)
    row = iota((EXTRA, HALF), 0)
    left = (row == 0) | (row == 2) | (row == 4)
    meta = jnp.where(row < 6, jnp.where(left, wide[:, :HALF], wide[:, HALF:]), first)
    out_ref[2 * TOK :, :] = meta.astype(BF)


def me_index():
    return lax.axis_index("z") * 4 + lax.axis_index("x")


def weights_of(s, old):
    top = jnp.ceil(jnp.max(s, axis=0, keepdims=True) * COEF)
    new = top if old is None else jnp.maximum(old, top)
    return new, jnp.exp2(s * COEF - new).astype(BF)


def verify_update(s, v_t, m_ref, l_ref, acc_ref, start=False):
    rows, keys = s.shape
    new = jnp.broadcast_to(jnp.ceil(jnp.max(s, axis=1, keepdims=True)), (rows, WIDTH))
    if not start:
        old = m_ref[...]
        new = jnp.maximum(old, new)
    p = jnp.exp2(s - jnp.tile(new, (1, keys // WIDTH)))
    mass = jnp.broadcast_to(jnp.sum(p, axis=1, keepdims=True), (rows, WIDTH))
    numer = dot_t(p.astype(BF), v_t)
    if not start:
        factor = jnp.exp2(old - new)
        mass = mass + l_ref[...] * factor
        numer = numer + acc_ref[...] * factor
    m_ref[...] = new
    l_ref[...] = mass
    acc_ref[...] = numer


def clipped_source(src_ref, base, col, mine, kc_ref, vc_ref, slot, ck_ref, cv_ref, b_ref):
    wide = src_ref[base + 2 * TOK : base + PAY, :].astype(F32)
    limit = slot * PAGES
    near = iota((PAGES // 2, HALF), 1) == 8 * iota((PAGES // 2, HALF), 0)
    picks = [jnp.where(near, wide[h : h + 1, :], 0.0) for h in range(2)]
    b_ref[limit : limit + PAGES, :] = dot(
        jnp.concatenate(picks, axis=0).astype(BF), jnp.ones((HALF, WIDTH), BF)
    )
    place = iota((2, HALF), 1) // 8 + 16 * iota((2, HALF), 0)
    hit = wide[4:6, :] == mine.astype(F32)
    page = jnp.max(jnp.where(hit, place, 0).astype(F32)).astype(jnp.int32)
    at = pl.ds(pl.multiple_of(col * 8, 8), 8)
    x = src_ref[base : base + TOK, :].astype(F32)
    pieces = []
    for p in range(PAGES):
        row = b_ref[pl.ds(limit + p, 8, stride=0), :]
        pieces.append(jnp.maximum(jnp.minimum(x[p * 8 : p * 8 + 8, :], row), -row))
    kc_ref[slot * TOK : (slot + 1) * TOK, :] = jnp.concatenate(pieces, axis=0).astype(BF)
    top = b_ref[pl.ds(limit + page, 8, stride=0), :]
    got = src_ref[pl.ds(pl.multiple_of(base + page * 8, 8), 8), :].astype(F32)
    ck_ref[at, :] = jnp.maximum(jnp.minimum(got, top), -top)
    total = None
    for h in range(2):
        raw = base + TOK + h * HALF
        row = wide[2 + h : 3 + h, :]
        x = src_ref[raw : raw + HALF, :].astype(F32)
        x = jnp.maximum(jnp.minimum(x, row), -row).astype(BF)
        vc_ref[2 * slot + h] = x
        one = iota((8, HALF), 1) + h * HALF == page * 8 + iota((8, HALF), 0)
        part = dot_t(one.astype(F32).astype(BF), x)
        total = part if total is None else total + part
    cv_ref[at, :] = total


def first_of(src_ref, base):
    meta = src_ref[base + 2 * TOK : base + PAY, :].astype(F32)
    return jnp.max(meta[8:, :]).astype(jnp.int32)


def joined(ref, first, count):
    return jnp.concatenate([ref[first + i] for i in range(count)], axis=1)


def own_kernel(
    q_ref, own_ref, dq_ref, tree_ref, far_ref, par_ref,
    m_ref, acc_ref, mv_ref, lv_ref, av_ref, ck_ref, cv_ref,
    kc_ref, vc_ref, b_ref,
):
    me = me_index()
    side = lax.axis_index("side")
    first = first_of(own_ref, 0)
    swap = (first >= PAGES).astype(jnp.int32)
    lo = pl.multiple_of(swap * HALF, HALF)
    hi = pl.multiple_of(HALF - swap * HALF, HALF)
    ones = jnp.ones((EXTRA, HALF), BF)
    k_lo, k_hi = own_ref[pl.ds(lo, HALF), :], own_ref[pl.ds(hi, HALF), :]
    v_lo = own_ref[pl.ds(pl.multiple_of(TOK + lo, HALF), HALF), :]
    v_hi = own_ref[pl.ds(pl.multiple_of(TOK + hi, HALF), HALF), :]
    v_lo = jnp.concatenate([v_lo, ones], axis=0)
    v_hi = jnp.concatenate([v_hi, ones], axis=0)
    k_both = jnp.concatenate([k_lo, k_hi], axis=0)
    v_both = jnp.concatenate([v_lo, v_hi], axis=1)
    for t in range(QH // PART):
        cols = slice(t * PART, (t + 1) * PART)
        token = iota((HALF, PART), 1) // GROUPS + t * PART // GROUPS
        open_ = iota((HALF, PART), 0) <= token
        q = q_ref[pl.ds(pl.multiple_of(hi * GROUPS + t * PART, PART), PART), :]
        s = dot_t(k_both, q)
        s = jnp.concatenate([s[:HALF], jnp.where(open_, s[HALF:], NEG)], axis=0)
        new, p = weights_of(s, None)
        acc_ref[1, :, cols] = dot(v_both, p)
        m_ref[1, :, cols] = jnp.broadcast_to(new, (8, PART))
        q = q_ref[pl.ds(pl.multiple_of(lo * GROUPS + t * PART, PART), PART), :]
        new, p = weights_of(jnp.where(open_, dot_t(k_lo, q), NEG), None)
        acc_ref[0, :, cols] = dot(v_lo, p)
        m_ref[0, :, cols] = jnp.broadcast_to(new, (8, PART))

    link = (par_ref[...] == iota((TOK, TOK), 0)) | (iota((TOK, TOK), 0) == iota((TOK, TOK), 1))
    link = link.astype(F32).astype(BF)
    for _ in range(8):
        link = jnp.minimum(dot(link, link), 1.0).astype(BF)
    rows64 = GROUPS * 8
    take = iota((rows64, TOK), 1) == me * 8 + iota((rows64, TOK), 0) // GROUPS
    allowed = dot_t(take.astype(F32).astype(BF), link) > 0.5

    def head(ref, at):
        zero, one = ref[:, at : at + WIDTH], ref[:, at + WIDTH : at + 2 * WIDTH]
        return jnp.where(side == 0, zero, one)

    def rows_of(at):
        near, far = head(tree_ref, at), head(far_ref, at)
        return jnp.concatenate(
            [jnp.where(side == 0, near, far), jnp.where(side == 0, far, near)], axis=0
        )

    dq = dq_ref[pl.ds(pl.multiple_of(me * rows64, rows64), rows64), :]
    s = jnp.where(allowed, dot_t(dq, rows_of(0)) * COEF, NEG)
    v_t = jnp.transpose(rows_of(2 * WIDTH).astype(F32)).astype(BF)
    verify_update(s, v_t, mv_ref, lv_ref, av_ref, start=True)
    clipped_source(own_ref, 0, me, me, kc_ref, vc_ref, 0, ck_ref, cv_ref, b_ref)
    verify_update(dot_t(dq, kc_ref[...]) * COEF, joined(vc_ref, 0, 2), mv_ref, lv_ref, av_ref)


def flash_chunks(q_ref, q_at, half, k_ref, v_ref, base, count, m_ref, acc_ref, s_ref):
    def chunk(slot, slots):
        span = slots * HALF
        k = k_ref[pl.ds(pl.multiple_of(slot * HALF, HALF), span), :]
        v = joined(v_ref, slot, slots)
        tiles = range(QH // PART)
        tops = []
        for t in tiles:
            q = q_ref[pl.ds(pl.multiple_of(q_at + t * PART, PART), PART), :]
            s = dot_t(k, q)
            s_ref[t, :span] = s
            tops.append(jnp.ceil(jnp.max(s, axis=0, keepdims=True) * COEF))
        for t in tiles:
            cols = slice(t * PART, (t + 1) * PART)
            old = m_ref[half, 0:1, cols]
            new = jnp.maximum(old, tops[t])
            p = jnp.exp2(s_ref[t, :span] * COEF - new).astype(BF)
            acc_ref[half, :, cols] = acc_ref[half, :, cols] * jnp.exp2(old - new) + dot(v, p)
            m_ref[half, :, cols] = jnp.broadcast_to(new, (8, PART))

    def full(i, _):
        chunk(base + i * SLOTS, SLOTS)
        return 0

    many = (count + 1) // SLOTS
    lax.fori_loop(0, many, full, 0)

    @pl.when(count > many * SLOTS)
    def _():
        chunk(base + many * SLOTS, SLOTS // 2)


def step_kernel(layout, last, *refs):
    n_in = len(layout)
    q_ref, own_ref, dq_ref = refs[:3]
    srcs = refs[3 : 3 + n_in]
    state = refs[3 + n_in + len(STATE) : 3 + n_in + 2 * len(STATE)]
    if last:
        out_ref, ver_ref, ok_ref, ov_ref = refs[3 + n_in + 2 * len(STATE) :][:4]
    kk_ref, vv_ref, kc_ref, vc_ref, b_ref, s_ref = refs[-6:]
    m_ref, acc_ref, mv_ref, lv_ref, av_ref, ck_ref, cv_ref = state
    me, z, x = me_index(), lax.axis_index("z"), lax.axis_index("x")
    first = first_of(own_ref, 0)
    swap = (first >= PAGES).astype(jnp.int32)
    mine = jnp.minimum(first, 2 * PAGES - 1 - first)
    blocks = [(r, i * PAY, d) for r, ds in zip(srcs, layout) for i, d in enumerate(ds)]
    n = len(blocks)
    lo_base = 2 * n + SLOTS
    ones = jnp.ones((EXTRA, HALF), BF)
    n_hi, n_lo = jnp.int32(0), jnp.int32(0)
    for i, (ref, base, _) in enumerate(blocks):
        f = first_of(ref, base)
        other = (f >= PAGES).astype(jnp.int32)
        later = (jnp.minimum(f, 2 * PAGES - 1 - f) > mine).astype(jnp.int32)
        lo = base + other * HALF
        hi = base + HALF - other * HALF
        sel = jnp.where(later == 1, hi, lo)
        to = jnp.where(later == 1, n + n_hi, lo_base + n_lo)
        kk_ref[i * HALF : (i + 1) * HALF, :] = ref[pl.ds(pl.multiple_of(lo, 16), HALF), :]
        vv_ref[i, :WIDTH, :] = ref[pl.ds(pl.multiple_of(lo + TOK, 16), HALF), :]
        vv_ref[i, WIDTH:, :] = ones
        at = pl.ds(pl.multiple_of(to * HALF, HALF), HALF)
        kk_ref[at, :] = ref[pl.ds(pl.multiple_of(sel, 16), HALF), :]
        vv_ref[to, :WIDTH, :] = ref[pl.ds(pl.multiple_of(sel + TOK, 16), HALF), :]
        vv_ref[to, WIDTH:, :] = ones
        n_hi, n_lo = n_hi + later, n_lo + 1 - later
    for start, count in ((0, n + n_hi), (lo_base, n_lo)):
        for j in range(1):
            at = pl.ds(pl.multiple_of((start + count + j) * HALF, HALF), HALF)
            kk_ref[at, :] = kk_ref[start * HALF : (start + 1) * HALF, :]
            vv_ref[start + count + j] = jnp.zeros((DEEP, HALF), BF)
    q_lo = swap * QH
    q_hi = QH - swap * QH

    def way(w, _):
        late = w == 0
        q_at = jnp.where(late, q_hi, q_lo)
        base = jnp.where(late, 0, lo_base)
        count = jnp.where(late, n + n_hi, n_lo)
        flash_chunks(q_ref, q_at, 1 - w, kk_ref, vv_ref, base, count, m_ref, acc_ref, s_ref)
        return 0

    lax.fori_loop(0, 2, way, 0)

    for i, (ref, base, (dz, dx)) in enumerate(blocks):
        col = ((z + dz + 8) % 8) * 4 + (x + dx + 4) % 4
        clipped_source(ref, base, col, me, kc_ref, vc_ref, i, ck_ref, cv_ref, b_ref)
    rows64 = GROUPS * 8
    dq = dq_ref[pl.ds(pl.multiple_of(me * rows64, rows64), rows64), :]
    verify_update(dot_t(dq, kc_ref[...]) * COEF, joined(vc_ref, 0, 2 * n), mv_ref, lv_ref, av_ref)
    if last:
        for t in range(QH // PART):
            cols = slice(t * PART, (t + 1) * PART)
            for at, half in ((q_hi, 1), (q_lo, 0)):
                a = acc_ref[half, :, cols]
                out = jnp.transpose(a[:WIDTH] / a[WIDTH : WIDTH + 1])
                out_ref[pl.ds(pl.multiple_of(at + t * PART, PART), PART), :] = out.astype(BF)
        ver_ref[...] = (av_ref[...] / lv_ref[...]).astype(BF)
        ok_ref[...] = ck_ref[...].astype(BF)
        ov_ref[...] = cv_ref[...].astype(BF)


STATE = [
    pltpu.VMEM((2, 8, QH), F32),
    pltpu.VMEM((2, DEEP, QH), F32),
    pltpu.VMEM((64, WIDTH), F32),
    pltpu.VMEM((64, WIDTH), F32),
    pltpu.VMEM((64, WIDTH), F32),
    pltpu.VMEM((TOK, WIDTH), F32),
    pltpu.VMEM((TOK, WIDTH), F32),
]
GRANT = pltpu.CompilerParams(vmem_limit_bytes=40 * 1024 * 1024)


def cost(n):
    return pl.CostEstimate(
        flops=n * 4 * TOK * QH * WIDTH, bytes_accessed=n * PAY * WIDTH * 2, transcendentals=0
    )


def step(q, own, dq, sources, layout, state, last=False):
    n = sum(len(d) for d in layout)
    outs = STATE
    alias = {3 + len(layout) + i: i for i in range(len(STATE))}
    if last:
        outs = STATE + [
            jax.ShapeDtypeStruct((2 * QH, WIDTH), BF),
            jax.ShapeDtypeStruct((64, WIDTH), BF),
            jax.ShapeDtypeStruct((TOK, WIDTH), BF),
            jax.ShapeDtypeStruct((TOK, WIDTH), BF),
        ]
    slots = 3 * n + 2 * SLOTS
    return pl.pallas_call(
        functools.partial(step_kernel, layout, last),
        out_shape=outs,
        in_specs=vmem(3 + len(layout) + len(STATE)),
        out_specs=vmem(len(outs)),
        scratch_shapes=[
            pltpu.VMEM((slots * HALF, WIDTH), BF),
            pltpu.VMEM((slots, DEEP, HALF), BF),
            pltpu.VMEM((n * TOK, WIDTH), BF),
            pltpu.VMEM((2 * n, HALF, WIDTH), BF),
            pltpu.VMEM((n * PAGES, WIDTH), F32),
            pltpu.VMEM((QH // PART, SLOTS * HALF, PART), F32),
        ],
        input_output_aliases=alias,
        cost_estimate=cost(n),
        compiler_params=GRANT,
    )(*(held(a) for a in (q, own, dq, *sources, *state)))


def shift(b, axis, d):
    n = lax.axis_size(axis)
    return lax.ppermute(b, axis, [(i, (i + d) % n) for i in range(n)])


def work(
    prefill_query, prefill_keys, prefill_values, token_pos, scale_exp, page_owner,
    draft_query, draft_keys, draft_values, parents,
):
    q = prefill_query.reshape(2 * QH, WIDTH)
    dq = draft_query.reshape(2 * QH, WIDTH)
    own = pl.pallas_call(
        pack_kernel,
        out_shape=pltpu.VMEM((PAY, WIDTH), BF),
        compiler_params=pltpu.CompilerParams(vmem_limit_bytes=4 * 1024 * 1024),
        in_specs=[pl.BlockSpec(memory_space=pl.ANY)] * 5,
        out_specs=vmem(1)[0],
        scratch_shapes=[
            pltpu.SMEM((TOK,), jnp.int32),
            pltpu.VMEM((2, PAGES), jnp.int32),
            pltpu.VMEM((1, PAGES), jnp.int32),
            pltpu.VMEM((TOK, WIDTH), BF),
            pltpu.SemaphoreType.DMA((5,)),
        ],
        name="pack",
    )(
        outside(token_pos),
        outside(jnp.transpose(scale_exp, (1, 2, 0)).reshape(2, PAGES)),
        outside(page_owner.reshape(1, PAGES)),
        outside(prefill_keys.reshape(TOK, WIDTH)),
        outside(prefill_values.reshape(TOK, WIDTH)),
    )
    tree = jnp.concatenate(
        [draft_keys.reshape(HALF, 2 * WIDTH), draft_values.reshape(HALF, 2 * WIDTH)], axis=1
    )
    xs = [shift(own, "x", 1), shift(own, "x", -1), shift(own, "x", 2)]
    far = shift(tree, "side", 1)
    near_x = jnp.concatenate(xs, axis=0)
    dxs = (-1, 1, 2)
    own_call = pl.pallas_call(
        own_kernel,
        out_shape=STATE,
        in_specs=vmem(6),
        out_specs=vmem(len(STATE)),
        scratch_shapes=[
            pltpu.VMEM((TOK, WIDTH), BF),
            pltpu.VMEM((2, HALF, WIDTH), BF),
            pltpu.VMEM((PAGES, WIDTH), F32),
        ],
        cost_estimate=cost(2),
        compiler_params=GRANT,
        name="own",
    )
    state = own_call(*(held(a) for a in (q, own, dq, tree, far, parents.reshape(1, TOK))))
    ra, la = shift(own, "z", 1), shift(own, "z", -1)
    state = step(
        q, own, dq, [near_x, ra, la],
        [[(0, d) for d in dxs], [(-1, 0)], [(1, 0)]],
        state,
    )
    rb = lb = near_x
    for s in range(1, 4):
        rb, lb = shift(rb, "z", 1), shift(lb, "z", -1)
        sources = [rb, lb]
        layout = [[(-s, d) for d in dxs], [(s, d) for d in dxs]]
        if s < 3:
            ra, la = shift(ra, "z", 1), shift(la, "z", -1)
            sources += [ra, la]
            layout += [[(-s - 1, 0)], [(s + 1, 0)]]
        state = step(q, own, dq, sources, layout, state)
    ob = shift(rb[: 2 * PAY], "z", 1)
    oa = shift(la, "z", -1)
    oc = shift(lb[2 * PAY :], "z", -1)
    out, ver, ck, cv = step(
        q, own, dq, [oa, ob, oc],
        [[(4, 0)], [(4, d) for d in dxs[:2]], [(4, dxs[2])]],
        state, last=True,
    )[len(STATE) :]
    return (
        out.reshape(TOK, GROUPS, WIDTH),
        ck.reshape(TOK, 1, WIDTH),
        cv.reshape(TOK, 1, WIDTH),
        ver.reshape(8, GROUPS, WIDTH),
    )


def solution(mesh):
    finer = Mesh(
        mesh.devices.reshape(8, 4, mesh.shape["head"], mesh.shape["side"]),
        ("z", "x", "head", "side"),
    )
    full = P(CTX, ("head", "side"), None)
    in_specs = (
        full, full, full, P(CTX), full, P(CTX),
        P(None, ("head", "side"), None),
        P("side", "head", None), P("side", "head", None), P(),
    )
    return jax.shard_map(
        work, mesh=finer, in_specs=in_specs, out_specs=(full, full, full, full), check_vma=False
    )
```

```python
import functools

import jax
import jax.numpy as jnp
from jax import lax
from jax.experimental import pallas as pl
from jax.experimental.pallas import tpu as pltpu
from jax.sharding import Mesh
from jax.sharding import PartitionSpec as P


CTX = ("z", "x")
NEG = -1.0e30
LOG_TWO_E = 1.4426950408889634
TOK = 256
HALF = 128
GROUPS = 8
WIDTH = 128
PAGES = 32
EXTRA = 16
PAY = 2 * TOK + EXTRA
DEEP = WIDTH + EXTRA
QH = HALF * GROUPS
SLOTS = 4
PART = 512
COEF = WIDTH**-0.5 * LOG_TWO_E
BF = jnp.bfloat16
F32 = jnp.float32


def iota(shape, dim):
    return lax.broadcasted_iota(jnp.int32, shape, dim)


def dot_t(a, b):
    return lax.dot_general(a, b, (((1,), (1,)), ((), ())), preferred_element_type=F32)


def dot(a, b):
    return jnp.dot(a, b, preferred_element_type=F32)


def outside(x):
    return pltpu.with_memory_space_constraint(x, pltpu.HBM)


def held(x):
    return pltpu.with_memory_space_constraint(x, pltpu.VMEM)


def vmem(n):
    return [pl.BlockSpec(memory_space=pltpu.VMEM)] * n


def pack_kernel(
    pos_hbm, scale_hbm, owner_hbm, k_hbm, v_hbm, out_ref, pos_ref, scale_ref, owner_ref, v_ref, sems
):
    copies = [
        pltpu.make_async_copy(a, b, sems.at[i])
        for i, (a, b) in enumerate(
            (
                (v_hbm, v_ref),
                (k_hbm, out_ref.at[0:TOK, :]),
                (pos_hbm, pos_ref),
                (scale_hbm, scale_ref),
                (owner_hbm, owner_ref),
            )
        )
    ]
    for c in copies:
        c.start()
    for c in copies:
        c.wait()
    v = jnp.transpose(v_ref[...].astype(F32)).astype(BF)
    out_ref[TOK : TOK + HALF, :] = v[:, :HALF]
    out_ref[TOK + HALF : 2 * TOK, :] = v[:, HALF:]
    first = (pos_ref[0] // HALF).astype(F32)
    scale = scale_ref[...]
    bound = jnp.where(scale == -7, 3.5, jnp.where(scale == -6, 7.0, 14.0)).astype(F32)
    own = owner_ref[...].astype(F32)
    grow = (iota((PAGES, TOK), 0) == iota((PAGES, TOK), 1) // 8).astype(F32).astype(BF)
    row = iota((EXTRA, PAGES), 0)
    few = jnp.where(row < 2, bound[0:1, :], jnp.where(row < 4, bound[1:2, :], own))
    wide = dot(few.astype(BF), grow)
    row = iota((EXTRA, HALF), 0)
    left = (row == 0) | (row == 2) | (row == 4)
    meta = jnp.where(row < 6, jnp.where(left, wide[:, :HALF], wide[:, HALF:]), first)
    out_ref[2 * TOK :, :] = meta.astype(BF)


def me_index():
    return lax.axis_index("z") * 4 + lax.axis_index("x")


def weights_of(s, old):
    top = jnp.ceil(jnp.max(s, axis=0, keepdims=True) * COEF)
    new = top if old is None else jnp.maximum(old, top)
    return new, jnp.exp2(s * COEF - new).astype(BF)


def verify_update(s, v_t, m_ref, l_ref, acc_ref, start=False):
    rows, keys = s.shape
    new = jnp.broadcast_to(jnp.ceil(jnp.max(s, axis=1, keepdims=True)), (rows, WIDTH))
    if not start:
        old = m_ref[...]
        new = jnp.maximum(old, new)
    p = jnp.exp2(s - jnp.tile(new, (1, keys // WIDTH)))
    mass = jnp.broadcast_to(jnp.sum(p, axis=1, keepdims=True), (rows, WIDTH))
    numer = dot_t(p.astype(BF), v_t)
    if not start:
        factor = jnp.exp2(old - new)
        mass = mass + l_ref[...] * factor
        numer = numer + acc_ref[...] * factor
    m_ref[...] = new
    l_ref[...] = mass
    acc_ref[...] = numer


def clipped_source(src_ref, base, col, mine, kc_ref, vc_ref, slot, ck_ref, cv_ref, b_ref):
    wide = src_ref[base + 2 * TOK : base + PAY, :].astype(F32)
    limit = slot * PAGES
    near = iota((PAGES // 2, HALF), 1) == 8 * iota((PAGES // 2, HALF), 0)
    picks = [jnp.where(near, wide[h : h + 1, :], 0.0) for h in range(2)]
    b_ref[limit : limit + PAGES, :] = dot(
        jnp.concatenate(picks, axis=0).astype(BF), jnp.ones((HALF, WIDTH), BF)
    )
    place = iota((2, HALF), 1) // 8 + 16 * iota((2, HALF), 0)
    hit = wide[4:6, :] == mine.astype(F32)
    page = jnp.max(jnp.where(hit, place, 0).astype(F32)).astype(jnp.int32)
    at = pl.ds(pl.multiple_of(col * 8, 8), 8)
    x = src_ref[base : base + TOK, :].astype(F32)
    pieces = []
    for p in range(PAGES):
        row = b_ref[pl.ds(limit + p, 8, stride=0), :]
        pieces.append(jnp.maximum(jnp.minimum(x[p * 8 : p * 8 + 8, :], row), -row))
    kc_ref[slot * TOK : (slot + 1) * TOK, :] = jnp.concatenate(pieces, axis=0).astype(BF)
    top = b_ref[pl.ds(limit + page, 8, stride=0), :]
    got = src_ref[pl.ds(pl.multiple_of(base + page * 8, 8), 8), :].astype(F32)
    ck_ref[at, :] = jnp.maximum(jnp.minimum(got, top), -top)
    total = None
    for h in range(2):
        raw = base + TOK + h * HALF
        row = wide[2 + h : 3 + h, :]
        x = src_ref[raw : raw + HALF, :].astype(F32)
        x = jnp.maximum(jnp.minimum(x, row), -row).astype(BF)
        vc_ref[2 * slot + h] = x
        one = iota((8, HALF), 1) + h * HALF == page * 8 + iota((8, HALF), 0)
        part = dot_t(one.astype(F32).astype(BF), x)
        total = part if total is None else total + part
    cv_ref[at, :] = total


def first_of(src_ref, base):
    meta = src_ref[base + 2 * TOK : base + PAY, :].astype(F32)
    return jnp.max(meta[8:, :]).astype(jnp.int32)


def joined(ref, first, count):
    return jnp.concatenate([ref[first + i] for i in range(count)], axis=1)


def own_kernel(q_ref, own_ref, m_ref, acc_ref):
    first = first_of(own_ref, 0)
    swap = (first >= PAGES).astype(jnp.int32)
    lo = pl.multiple_of(swap * HALF, HALF)
    hi = pl.multiple_of(HALF - swap * HALF, HALF)
    ones = jnp.ones((EXTRA, HALF), BF)
    k_lo, k_hi = own_ref[pl.ds(lo, HALF), :], own_ref[pl.ds(hi, HALF), :]
    v_lo = own_ref[pl.ds(pl.multiple_of(TOK + lo, HALF), HALF), :]
    v_hi = own_ref[pl.ds(pl.multiple_of(TOK + hi, HALF), HALF), :]
    v_lo = jnp.concatenate([v_lo, ones], axis=0)
    v_hi = jnp.concatenate([v_hi, ones], axis=0)
    k_both = jnp.concatenate([k_lo, k_hi], axis=0)
    v_both = jnp.concatenate([v_lo, v_hi], axis=1)
    for t in range(QH // PART):
        cols = slice(t * PART, (t + 1) * PART)
        token = iota((HALF, PART), 1) // GROUPS + t * PART // GROUPS
        open_ = iota((HALF, PART), 0) <= token
        q = q_ref[pl.ds(pl.multiple_of(hi * GROUPS + t * PART, PART), PART), :]
        s = dot_t(k_both, q)
        s = jnp.concatenate([s[:HALF], jnp.where(open_, s[HALF:], NEG)], axis=0)
        new, p = weights_of(s, None)
        acc_ref[1, :, cols] = dot(v_both, p)
        m_ref[1, :, cols] = jnp.broadcast_to(new, (8, PART))
        q = q_ref[pl.ds(pl.multiple_of(lo * GROUPS + t * PART, PART), PART), :]
        new, p = weights_of(jnp.where(open_, dot_t(k_lo, q), NEG), None)
        acc_ref[0, :, cols] = dot(v_lo, p)
        m_ref[0, :, cols] = jnp.broadcast_to(new, (8, PART))


def tree_kernel(own_ref, dq_ref, tree_ref, far_ref, par_ref, *refs):
    mv_ref, lv_ref, av_ref, ck_ref, cv_ref, kc_ref, vc_ref, b_ref = refs[5:]
    me = me_index()
    side = lax.axis_index("side")
    link = (par_ref[...] == iota((TOK, TOK), 0)) | (iota((TOK, TOK), 0) == iota((TOK, TOK), 1))
    link = link.astype(F32).astype(BF)
    for _ in range(8):
        link = jnp.minimum(dot(link, link), 1.0).astype(BF)
    rows64 = GROUPS * 8
    take = iota((rows64, TOK), 1) == me * 8 + iota((rows64, TOK), 0) // GROUPS
    allowed = dot_t(take.astype(F32).astype(BF), link) > 0.5

    def head(ref, at):
        zero, one = ref[:, at : at + WIDTH], ref[:, at + WIDTH : at + 2 * WIDTH]
        return jnp.where(side == 0, zero, one)

    def rows_of(at):
        near, far = head(tree_ref, at), head(far_ref, at)
        return jnp.concatenate(
            [jnp.where(side == 0, near, far), jnp.where(side == 0, far, near)], axis=0
        )

    dq = dq_ref[pl.ds(pl.multiple_of(me * rows64, rows64), rows64), :]
    s = jnp.where(allowed, dot_t(dq, rows_of(0)) * COEF, NEG)
    v_t = jnp.transpose(rows_of(2 * WIDTH).astype(F32)).astype(BF)
    verify_update(s, v_t, mv_ref, lv_ref, av_ref)
    clipped_source(own_ref, 0, me, me, kc_ref, vc_ref, 0, ck_ref, cv_ref, b_ref)
    verify_update(dot_t(dq, kc_ref[...]) * COEF, joined(vc_ref, 0, 2), mv_ref, lv_ref, av_ref)


def flash_chunks(q_ref, q_at, half, k_ref, v_ref, base, count, m_ref, acc_ref, s_ref):
    def chunk(slot, slots):
        span = slots * HALF
        k = k_ref[pl.ds(pl.multiple_of(slot * HALF, HALF), span), :]
        v = joined(v_ref, slot, slots)
        tiles = range(QH // PART)
        tops = []
        for t in tiles:
            q = q_ref[pl.ds(pl.multiple_of(q_at + t * PART, PART), PART), :]
            s = dot_t(k, q)
            s_ref[t, :span] = s
            tops.append(jnp.ceil(jnp.max(s, axis=0, keepdims=True) * COEF))
        for t in tiles:
            cols = slice(t * PART, (t + 1) * PART)
            old = m_ref[half, 0:1, cols]
            new = jnp.maximum(old, tops[t])
            p = jnp.exp2(s_ref[t, :span] * COEF - new).astype(BF)
            acc_ref[half, :, cols] = acc_ref[half, :, cols] * jnp.exp2(old - new) + dot(v, p)
            m_ref[half, :, cols] = jnp.broadcast_to(new, (8, PART))

    def full(i, _):
        chunk(base + i * SLOTS, SLOTS)
        return 0

    many = (count + 1) // SLOTS
    lax.fori_loop(0, many, full, 0)

    @pl.when(count > many * SLOTS)
    def _():
        chunk(base + many * SLOTS, SLOTS // 2)


def step_kernel(layout, place, *refs):
    n_in = len(layout)
    first_call, last = place == 0, place == 2
    held_in = 2 if first_call else len(STATE)
    q_ref, own_ref, dq_ref = refs[:3]
    srcs = refs[3 : 3 + n_in]
    state = refs[3 + n_in + held_in : 3 + n_in + held_in + len(STATE)]
    if last:
        out_ref, ver_ref, ok_ref, ov_ref = refs[3 + n_in + 2 * len(STATE) :][:4]
    kk_ref, vv_ref, kc_ref, vc_ref, b_ref, s_ref = refs[-6:]
    m_ref, acc_ref, mv_ref, lv_ref, av_ref, ck_ref, cv_ref = state
    me, z, x = me_index(), lax.axis_index("z"), lax.axis_index("x")
    first = first_of(own_ref, 0)
    swap = (first >= PAGES).astype(jnp.int32)
    mine = jnp.minimum(first, 2 * PAGES - 1 - first)
    blocks = [(r, i * PAY, d) for r, ds in zip(srcs, layout) for i, d in enumerate(ds)]
    n = len(blocks)
    lo_base = 2 * n + SLOTS
    ones = jnp.ones((EXTRA, HALF), BF)
    n_hi, n_lo = jnp.int32(0), jnp.int32(0)
    for i, (ref, base, _) in enumerate(blocks):
        f = first_of(ref, base)
        other = (f >= PAGES).astype(jnp.int32)
        later = (jnp.minimum(f, 2 * PAGES - 1 - f) > mine).astype(jnp.int32)
        lo = base + other * HALF
        hi = base + HALF - other * HALF
        sel = jnp.where(later == 1, hi, lo)
        to = jnp.where(later == 1, n + n_hi, lo_base + n_lo)
        kk_ref[i * HALF : (i + 1) * HALF, :] = ref[pl.ds(pl.multiple_of(lo, 16), HALF), :]
        vv_ref[i, :WIDTH, :] = ref[pl.ds(pl.multiple_of(lo + TOK, 16), HALF), :]
        vv_ref[i, WIDTH:, :] = ones
        at = pl.ds(pl.multiple_of(to * HALF, HALF), HALF)
        kk_ref[at, :] = ref[pl.ds(pl.multiple_of(sel, 16), HALF), :]
        vv_ref[to, :WIDTH, :] = ref[pl.ds(pl.multiple_of(sel + TOK, 16), HALF), :]
        vv_ref[to, WIDTH:, :] = ones
        n_hi, n_lo = n_hi + later, n_lo + 1 - later
    for start, count in ((0, n + n_hi), (lo_base, n_lo)):
        for j in range(1):
            at = pl.ds(pl.multiple_of((start + count + j) * HALF, HALF), HALF)
            kk_ref[at, :] = kk_ref[start * HALF : (start + 1) * HALF, :]
            vv_ref[start + count + j] = jnp.zeros((DEEP, HALF), BF)
    q_lo = swap * QH
    q_hi = QH - swap * QH

    def way(w, _):
        late = w == 0
        q_at = jnp.where(late, q_hi, q_lo)
        base = jnp.where(late, 0, lo_base)
        count = jnp.where(late, n + n_hi, n_lo)
        flash_chunks(q_ref, q_at, 1 - w, kk_ref, vv_ref, base, count, m_ref, acc_ref, s_ref)
        return 0

    lax.fori_loop(0, 2, way, 0)

    for i, (ref, base, (dz, dx)) in enumerate(blocks):
        col = ((z + dz + 8) % 8) * 4 + (x + dx + 4) % 4
        clipped_source(ref, base, col, me, kc_ref, vc_ref, i, ck_ref, cv_ref, b_ref)
    rows64 = GROUPS * 8
    dq = dq_ref[pl.ds(pl.multiple_of(me * rows64, rows64), rows64), :]
    s = dot_t(dq, kc_ref[...]) * COEF
    verify_update(s, joined(vc_ref, 0, 2 * n), mv_ref, lv_ref, av_ref, start=first_call)
    if last:
        for t in range(QH // PART):
            cols = slice(t * PART, (t + 1) * PART)
            for at, half in ((q_hi, 1), (q_lo, 0)):
                a = acc_ref[half, :, cols]
                out = jnp.transpose(a[:WIDTH] / a[WIDTH : WIDTH + 1])
                out_ref[pl.ds(pl.multiple_of(at + t * PART, PART), PART), :] = out.astype(BF)
        ver_ref[...] = (av_ref[...] / lv_ref[...]).astype(BF)
        ok_ref[...] = ck_ref[...].astype(BF)
        ov_ref[...] = cv_ref[...].astype(BF)


STATE = [
    pltpu.VMEM((2, 8, QH), F32),
    pltpu.VMEM((2, DEEP, QH), F32),
    pltpu.VMEM((64, WIDTH), F32),
    pltpu.VMEM((64, WIDTH), F32),
    pltpu.VMEM((64, WIDTH), F32),
    pltpu.VMEM((TOK, WIDTH), F32),
    pltpu.VMEM((TOK, WIDTH), F32),
]
GRANT = pltpu.CompilerParams(vmem_limit_bytes=40 * 1024 * 1024)


def cost(n):
    return pl.CostEstimate(
        flops=n * 4 * TOK * QH * WIDTH, bytes_accessed=n * PAY * WIDTH * 2, transcendentals=0
    )


def step(q, own, dq, sources, layout, state, place=1):
    n = sum(len(d) for d in layout)
    outs = STATE
    alias = {3 + len(layout) + i: i for i in range(len(state))}
    if place == 2:
        outs = STATE + [
            jax.ShapeDtypeStruct((2 * QH, WIDTH), BF),
            jax.ShapeDtypeStruct((64, WIDTH), BF),
            jax.ShapeDtypeStruct((TOK, WIDTH), BF),
            jax.ShapeDtypeStruct((TOK, WIDTH), BF),
        ]
    slots = 3 * n + 2 * SLOTS
    return pl.pallas_call(
        functools.partial(step_kernel, layout, place),
        out_shape=outs,
        in_specs=vmem(3 + len(layout) + len(state)),
        out_specs=vmem(len(outs)),
        scratch_shapes=[
            pltpu.VMEM((slots * HALF, WIDTH), BF),
            pltpu.VMEM((slots, DEEP, HALF), BF),
            pltpu.VMEM((n * TOK, WIDTH), BF),
            pltpu.VMEM((2 * n, HALF, WIDTH), BF),
            pltpu.VMEM((n * PAGES, WIDTH), F32),
            pltpu.VMEM((QH // PART, SLOTS * HALF, PART), F32),
        ],
        input_output_aliases=alias,
        cost_estimate=cost(n),
        compiler_params=GRANT,
    )(*(held(a) for a in (q, own, dq, *sources, *state)))


def shift(b, axis, d):
    n = lax.axis_size(axis)
    return lax.ppermute(b, axis, [(i, (i + d) % n) for i in range(n)])


def work(
    prefill_query, prefill_keys, prefill_values, token_pos, scale_exp, page_owner,
    draft_query, draft_keys, draft_values, parents,
):
    q = prefill_query.reshape(2 * QH, WIDTH)
    dq = draft_query.reshape(2 * QH, WIDTH)
    own = pl.pallas_call(
        pack_kernel,
        out_shape=pltpu.VMEM((PAY, WIDTH), BF),
        compiler_params=pltpu.CompilerParams(vmem_limit_bytes=4 * 1024 * 1024),
        in_specs=[pl.BlockSpec(memory_space=pl.ANY)] * 5,
        out_specs=vmem(1)[0],
        scratch_shapes=[
            pltpu.SMEM((TOK,), jnp.int32),
            pltpu.VMEM((2, PAGES), jnp.int32),
            pltpu.VMEM((1, PAGES), jnp.int32),
            pltpu.VMEM((TOK, WIDTH), BF),
            pltpu.SemaphoreType.DMA((5,)),
        ],
        name="pack",
    )(
        outside(token_pos),
        outside(jnp.transpose(scale_exp, (1, 2, 0)).reshape(2, PAGES)),
        outside(page_owner.reshape(1, PAGES)),
        outside(prefill_keys.reshape(TOK, WIDTH)),
        outside(prefill_values.reshape(TOK, WIDTH)),
    )
    tree = jnp.concatenate(
        [draft_keys.reshape(HALF, 2 * WIDTH), draft_values.reshape(HALF, 2 * WIDTH)], axis=1
    )
    xs = [shift(own, "x", 1), shift(own, "x", -1), shift(own, "x", 2)]
    far = shift(tree, "side", 1)
    near_x = jnp.concatenate(xs, axis=0)
    dxs = (-1, 1, 2)
    own_call = pl.pallas_call(
        own_kernel,
        out_shape=STATE[:2],
        in_specs=vmem(2),
        out_specs=vmem(2),
        cost_estimate=cost(2),
        compiler_params=GRANT,
        name="own",
    )
    state = own_call(held(q), held(own))
    tree_call = pl.pallas_call(
        tree_kernel,
        out_shape=STATE[2:],
        in_specs=vmem(10),
        out_specs=vmem(5),
        scratch_shapes=[
            pltpu.VMEM((TOK, WIDTH), BF),
            pltpu.VMEM((2, HALF, WIDTH), BF),
            pltpu.VMEM((PAGES, WIDTH), F32),
        ],
        input_output_aliases={5 + i: i for i in range(5)},
        cost_estimate=cost(2),
        compiler_params=GRANT,
        name="tree",
    )
    ra, la = shift(own, "z", 1), shift(own, "z", -1)
    state = step(
        q, own, dq, [near_x, ra, la],
        [[(0, d) for d in dxs], [(-1, 0)], [(1, 0)]],
        state, place=0,
    )
    rb = lb = near_x
    for s in range(1, 4):
        rb, lb = shift(rb, "z", 1), shift(lb, "z", -1)
        sources = [rb, lb]
        layout = [[(-s, d) for d in dxs], [(s, d) for d in dxs]]
        if s < 3:
            ra, la = shift(ra, "z", 1), shift(la, "z", -1)
            sources += [ra, la]
            layout += [[(-s - 1, 0)], [(s + 1, 0)]]
        state = step(q, own, dq, sources, layout, state)
        if s == 2:
            ver = tree_call(
                *(held(a) for a in (own, dq, tree, far, parents.reshape(1, TOK), *state[2:]))
            )
            state = [*state[:2], *ver]
    ob = shift(rb[: 2 * PAY], "z", 1)
    oa = shift(la, "z", -1)
    oc = shift(lb[2 * PAY :], "z", -1)
    out, ver, ck, cv = step(
        q, own, dq, [oa, ob, oc],
        [[(4, 0)], [(4, d) for d in dxs[:2]], [(4, dxs[2])]],
        state, place=2,
    )[len(STATE) :]
    return (
        out.reshape(TOK, GROUPS, WIDTH),
        ck.reshape(TOK, 1, WIDTH),
        cv.reshape(TOK, 1, WIDTH),
        ver.reshape(8, GROUPS, WIDTH),
    )


def solution(mesh):
    finer = Mesh(
        mesh.devices.reshape(8, 4, mesh.shape["head"], mesh.shape["side"]),
        ("z", "x", "head", "side"),
    )
    full = P(CTX, ("head", "side"), None)
    in_specs = (
        full, full, full, P(CTX), full, P(CTX),
        P(None, ("head", "side"), None),
        P("side", "head", None), P("side", "head", None), P(),
    )
    return jax.shard_map(
        work, mesh=finer, in_specs=in_specs, out_specs=(full, full, full, full), check_vma=False
    )
```
